128 devices in a mesh: px: 8 (over z, core), pz: 16 (over x, y).
Axes of the slice: x: 4, y: 4, z: 4, core: 2. Of those that a mesh axis runs over, the one named last changes fastest.
Arguments:
- charge: float32 [32768, 128], P(('px', 'pz')), may hold values from -6 to 6
- dest: int32 [32768, 1], P(('px', 'pz')), may hold values from 0 to 127; in each aligned block of 256 rows (0 to 255, 256 to 511, ...) at most 4 rows name the same one
- local_ids: int32 [32768], P(('px', 'pz')), may hold values from 0 to 255
- green_hat: float32 [128, 128, 2048], P(None, 'px', 'pz'), may hold values from 0.1 to 10, as said below
Outputs:
- potential: float32 [32768, 128], P(('px', 'pz'))
The draws below stay inside these ranges and needn't reach their ends.
Inputs may be any that keep to these rules, and one draw needn't show every extreme that they name: `dest`: among the 256 slots of one box, no pencil is named by more than 4; some pencil is named by exactly 4. green_hat is even in every dimension: its value at frequencies (k1, k2, k3) equals that at ((128 - k1) mod 2 * 64, (128 - k2) mod 2 * 64, (2048 - k3) mod 2 * 1024) taken in any single dimension.
All inputs are finite; a program needn't handle non-finite values.
Results may differ from the reference program's by a relative error of at most 0.00007.
Values sent between devices are 32-bit elements; how exact they have to be, the bound alone decides.
No kernel may reach another device: no remote copies, remote signals or barrier semaphores. Data moves between devices by JAX's collectives and lax.ppermute only.
A program may use at most 64 MiB of HBM per device.

```python
import math
import jax
import jax.numpy as jnp
import numpy as np

CXP = 8
CYP = 4
NZP = 1024
SLOTS = 256
PBLK = 256
CAP = 4
NX = 64
NY = 64
N_PX = 8
N_PZ = 16
DEVICES = 128


def mirror_mean(values, axis_number):
    length = values.shape[axis_number]
    mirrored_index = (length - jnp.arange(length, dtype=jnp.int32)) % length
    return 0.5 * (values + jnp.take(values, mirrored_index, axis=axis_number))


def draw_green_hat(key, part):
    shape = (2 * NX, 2 * NY, 2 * NZP)
    values = jax.random.uniform(key, shape, jnp.float32, 0.1, 10.0)
    values = mirror_mean(values, 0)
    values = mirror_mean(values, 1)
    values = mirror_mean(values, 2)
    return values.astype(jnp.float32)


def set_ends(drawn, key, low, top_value):
    longest = drawn.shape.index(max(drawn.shape))
    spots = []
    for shift in (0, 1):
        where = [jax.random.randint(jax.random.fold_in(key, axis), (), 0, length) for axis, length in enumerate(drawn.shape)]
        where[longest] = (where[longest] + shift) % drawn.shape[longest]
        spots.append(tuple(where))
    return drawn.at[spots[0]].set(low).at[spots[1]].set(top_value)


def level_of(rng, extent, pieces, smallest, high):
    gain = 1.0
    for axis_at, shards_of in pieces:
        draws = jax.random.uniform(jax.random.fold_in(jax.random.fold_in(rng, 6), axis_at), (shards_of,), jnp.float32, smallest / len(pieces), high / len(pieces))
        gain = gain * jnp.repeat(jnp.exp(draws), extent[axis_at] // shards_of).reshape((-1,) + (1,) * (len(extent) - 1 - axis_at))
    return gain


def shared_out(key, own, number, rows, count, top, most, skew):
    order = jax.random.permutation(key, count)
    heavy_load, ordinary = shares(count, rows * top, most, skew, True), shares(count, rows * top, most, skew, False)
    places = jnp.arange(count)

    def named(lengths, rotation):
        used = int((lengths > 0).sum())
        fixed = max(1, used // 4)
        moved = fixed + (places - fixed + rotation * (used - fixed)) % max(1, count - fixed)
        return jnp.zeros((count,), jnp.int32).at[order[jnp.where(places < fixed, places, moved)]].set(jnp.asarray(lengths, jnp.int32))

    lengths = jnp.where(number % 4 == 0, named(heavy_load, number // 4), named(ordinary, number - number // 4 - 1))
    mixed = jax.random.permutation(jax.random.fold_in(own, 3), count)
    donor, taker = mixed[0:count // 2 * 2:2], mixed[1:count // 2 * 2:2]
    room = jnp.minimum(lengths[donor] - 1, most - lengths[taker]) // 2
    room = jnp.where((donor == order[0]) | (taker == order[0]) | (lengths[taker] == 0), 0, jnp.maximum(room, 0))
    moved = jax.random.randint(jax.random.fold_in(own, 4), (count // 2,), 0, 1 << 20) % (room + 1)
    lengths = lengths.at[donor].add(-moved).at[taker].add(moved)
    items = jnp.searchsorted(jnp.cumsum(lengths), jnp.arange(rows * top), side="right").astype(jnp.int32)
    listing = items.reshape(top, rows).T
    listing = listing[jax.random.permutation(jax.random.fold_in(own, 1), rows)]
    rotation = jax.random.randint(jax.random.fold_in(own, 2), (rows, 1), 0, top)
    return jnp.take_along_axis(listing, (jnp.arange(top)[None, :] + rotation) % top, axis=1)


def shares(count, total, limit, skew, full):
    weights = [(1 << 20) // math.isqrt(grade ** skew) + 1 for grade in range(1, count + 1)]
    largest = limit if full else min(limit, max(-(-total // count), total * weights[0] // sum(weights)))
    least = 1 if total - largest >= count - 1 else 0
    holding, surplus = [largest] + [least] * (count - 1), total - largest - least * (count - 1)
    while surplus > 0:
        free = [i for i in range(1, count) if holding[i] < largest] or [i for i in range(1, count) if holding[i] < limit]
        mass, budget = sum([weights[i] for i in free]), surplus
        for i in free:
            extra = min(limit - holding[i], max(1, budget * weights[i] // mass), surplus)
            holding[i] = holding[i] + extra
            surplus = surplus - extra
    return np.array(holding)


def noise(stream_key, dims, scale, bound, pieces=(), held_as=jnp.bfloat16):
    drawn = jax.random.normal(stream_key, dims, jnp.float32) * scale
    if len(pieces) > 0:
        drawn = level_of(stream_key, dims, pieces, -0.22, 0.18) * drawn
    return jnp.clip(drawn, min=-bound, max=bound).astype(held_as)


def setup_inputs(seed: int = 0) -> dict:
    key_of = jax.random.split(jax.random.key(seed), 5)
    charge = noise(key_of[0], (DEVICES * SLOTS, 128), 1.0, 6.0, ((0, 128),), jnp.float32)
    dest_keys = jax.random.split(jax.random.fold_in(key_of[1], 1), (DEVICES * SLOTS) // SLOTS)
    dest_turns = jax.random.permutation(jax.random.fold_in(key_of[1], 3), (DEVICES * SLOTS) // SLOTS)
    dest = jax.vmap(lambda own, number: shared_out(jax.random.fold_in(key_of[1], 2), own, number, SLOTS, DEVICES, 1, CAP, 2))(dest_keys, dest_turns).reshape((DEVICES * SLOTS, 1))
    local_ids = set_ends(jax.random.randint(key_of[2], (DEVICES * SLOTS,), 0, PBLK), jax.random.fold_in(key_of[2], 1), 0, PBLK - 1).astype(jnp.int32)
    green_hat = draw_green_hat(jax.random.fold_in(key_of[4], 71), 0)
    return dict(charge=charge, dest=dest, local_ids=local_ids, green_hat=green_hat)


def reference(charge, dest, local_ids, green_hat):
    wide_x = CXP * N_PX
    wide_y = CYP * N_PZ
    target = dest[:, 0] * PBLK + local_ids
    blocks = jax.ops.segment_sum(charge, target, num_segments=DEVICES * PBLK)
    grid = blocks.reshape(N_PX, N_PZ, CXP, CYP, NZP).transpose(0, 2, 1, 3, 4).reshape(wide_x, wide_y, NZP)
    padded = jnp.zeros((2 * wide_x, 2 * wide_y, 2 * NZP), jnp.float32).at[:wide_x, :wide_y, :NZP].set(grid)
    spectrum = jnp.fft.fftn(padded)
    phi = jnp.real(jnp.fft.ifftn(spectrum * green_hat))[:wide_x, :wide_y, :NZP].astype(jnp.float32)
    back = phi.reshape(N_PX, CXP, N_PZ, CYP, NZP).transpose(0, 2, 1, 3, 4).reshape(DEVICES * PBLK, 128)
    return back[target]
```

```python
import jax
import jax.numpy as jnp
import ml_dtypes
import numpy as np
from jax import lax
from jax.experimental import pallas as pl
from jax.experimental.pallas import tpu as pltpu
from jax.sharding import PartitionSpec as P

CXP = 8
CYP = 4
CAP = 4
N_PX = 8
N_PZ = 16
N_DEV = 128
BOTH = ("px", "pz")
RESIDUE = [0, 8] + [g for g in range(1, 8) for _ in range(2)]
BF = jnp.bfloat16
F32 = jnp.float32
VMEM = pl.BlockSpec(memory_space=pltpu.VMEM)
PARAMS = pltpu.CompilerParams(vmem_limit_bytes=48 << 20)


def split_table(table):
    high = table.astype(np.float32).astype(ml_dtypes.bfloat16)
    low = (table - high.astype(np.float64)).astype(ml_dtypes.bfloat16)
    return high, low


def z_tables():
    device = np.arange(N_DEV)
    q = 8 * (device % N_PZ) + device // N_PZ
    l = np.arange(128)
    wave = []
    for r in range(9):
        angle = 2.0 * np.pi * ((q[:, None] * 16 + r) * l[None, :] % 2048) / 2048.0
        wave.append(np.concatenate([np.cos(angle), np.sin(angle)], axis=1))
    wave = np.stack(wave)
    mix = np.zeros((8, 4, 8, 2, 4, 16, 8))
    for c in range(8):
        for kk in range(16):
            r = RESIDUE[kk]
            angle = 2.0 * np.pi * ((r * c) % 16) / 16.0
            if kk < 2:
                cosine_part, sine_part, weight = np.cos(angle), np.cos(angle), 1.0
            elif kk % 2 == 0:
                cosine_part, sine_part, weight = np.cos(angle), -np.sin(angle), 2.0
            else:
                cosine_part, sine_part, weight = np.sin(angle), np.cos(angle), 2.0
            scale = np.sqrt(weight / 2048.0)
            for b in range(4):
                for a in range(8):
                    mix[c, b, a, 0, b, kk, a] = cosine_part * scale
                    mix[c, b, a, 1, b, kk, a] = sine_part * scale
    return wave, mix.reshape(256, 1024)


def plane_table():
    angle = 2.0 * np.pi * (np.arange(64)[:, None] * np.arange(128)[None, :] % 128) / 128.0
    return (np.cos(angle) + np.sin(angle)) / np.sqrt(128.0)


def iota(shape, axis):
    return lax.broadcasted_iota(jnp.int32, shape, axis)


def two(x):
    high = x.astype(BF)
    return high, (x - high.astype(F32)).astype(BF)


def three(x):
    high = x.astype(BF)
    rest = x - high.astype(F32)
    middle = rest.astype(BF)
    return high, middle, (rest - middle.astype(F32)).astype(BF)


def dot(a, b, a_axis=1, b_axis=0):
    return lax.dot_general(a, b, (((a_axis,), (b_axis,)), ((), ())), preferred_element_type=F32)


def pack_kernel(charge_ref, dest_ref, ids_ref, send_ref, place_ref):
    dest = jnp.broadcast_to(dest_ref[...], (256, 256))
    row, col = iota((256, 256), 0), iota((256, 256), 1)
    dest_f = dest.astype(F32)
    dest_col = jnp.sum(jnp.where(row == col, dest_f, 0.0), axis=1, keepdims=True)
    earlier = (dest_col == dest_f) & (row < col)
    rank = jnp.sum(jnp.where(earlier, 1.0, 0.0), axis=0, keepdims=True)
    place_ref[...] = dest_f[0:1] * CAP + rank
    here = iota((128, 256), 0) == dest[:128]
    rank = jnp.broadcast_to(rank, (128, 256))
    ids = jnp.broadcast_to(ids_ref[...], (128, 256)).astype(F32)
    lane = iota((128, 128), 1)
    named = jnp.zeros((128, 128), F32)
    hots = []
    for slot in range(CAP):
        chosen = here & (rank == slot)
        hots.append(jnp.where(chosen, 1.0, 0.0).astype(BF))
        number = jnp.sum(jnp.where(chosen, ids + 1.0, 0.0), axis=1, keepdims=True) - 1.0
        named = jnp.where(lane == slot, number, named)
    parts = jnp.concatenate(three(charge_ref[...]), axis=1)
    moved = dot(jnp.concatenate(hots, axis=0), parts)
    moved = moved[:, :128] + moved[:, 128:256] + moved[:, 256:]
    for slot in range(CAP):
        send_ref[pl.ds(slot, 128, stride=5), :] = moved[slot * 128 : (slot + 1) * 128]
    send_ref[pl.ds(4, 128, stride=5), :] = named


def slot_hots(recv_ref):
    lane = iota((128, 256), 1)
    block = ((lane % 8) * 4 + (lane // 8) % 4) * 8 + lane // 32
    block = block.astype(F32)
    names = recv_ref[pl.ds(4, 128, stride=5), :]
    hots = [jnp.where(names[:, s : s + 1] == block, 1.0, 0.0).astype(BF) for s in range(CAP)]
    return jnp.concatenate(hots, axis=0)


def lane_residue(shape):
    kk = (iota(shape, 1) // 8) % 16
    return jnp.where(kk == 0, 0, jnp.where(kk == 1, 8, kk // 2))


def z_forward_kernel(recv_ref, wave_hi_ref, wave_lo_ref, mix_hi_ref, mix_lo_ref, out_ref):
    hots = slot_hots(recv_ref)
    rows = jnp.concatenate([recv_ref[pl.ds(s, 128, stride=5), :] for s in range(CAP)], axis=0)
    parts = jnp.concatenate(three(rows), axis=1)
    field = dot(parts, hots, 0, 0)
    field = field[:128] + field[128:256] + field[256:]
    high, low = two(field)
    mixed = dot(high, mix_hi_ref[...]) + dot(low, mix_hi_ref[...]) + dot(high, mix_lo_ref[...])
    mixed = jnp.concatenate([mixed[:, :512], mixed[:, 512:]], axis=0)
    high, low = two(mixed)
    residue = lane_residue((128, 512))
    out = jnp.zeros((128, 512), F32)
    for r in range(9):
        rows = slice(r * 128, (r + 1) * 128)
        block = dot(wave_hi_ref[rows, :], high) + dot(wave_hi_ref[rows, :], low) + dot(wave_lo_ref[rows, :], high)
        out = jnp.where(residue == r, block, out)
    for b in range(CYP):
        out_ref[pl.ds(b, 128, stride=4), :] = out[:, b * 128 : (b + 1) * 128]


def plane_kernel(spec_ref, green_ref, fwd_ref, back_ref, back_lo_ref, out_ref, first_ref, second_ref):
    fwd = fwd_ref[...]
    back, back_lo = back_ref[...], back_lo_ref[...]
    for i in range(N_PX):
        high, low = two(spec_ref[i * 64 : (i + 1) * 64, :])
        turned = dot(jnp.concatenate([high, low, high], axis=0), fwd, 0, 0)
        for kk in range(16):
            first_ref[kk, i * 8 : (i + 1) * 8, :] = turned[kk * 8 : (kk + 1) * 8]
    for kk in range(16):
        high, low = two(first_ref[kk])
        full = dot(jnp.concatenate([high, low, high], axis=0), fwd, 0, 0)
        full = full * green_ref[pl.ds(RESIDUE[kk], 128, stride=16), :]
        high, low = two(full)
        second_ref[kk] = dot(back, jnp.concatenate([high, low], axis=1), 1, 1) + dot(back_lo, high, 1, 1)
    for i in range(N_PX):
        rows = jnp.concatenate([second_ref[kk, i * 8 : (i + 1) * 8, :] for kk in range(16)], axis=0)
        high, low = two(rows)
        out_ref[i * 64 : (i + 1) * 64, :] = dot(back, jnp.concatenate([high, low], axis=1), 1, 1) + dot(
            back_lo, high, 1, 1
        )


def z_back_kernel(spec_ref, recv_ref, wave_hi_ref, wave_lo_ref, mix_hi_ref, mix_lo_ref, out_ref):
    lines = jnp.concatenate([spec_ref[pl.ds(b, 128, stride=4), :] for b in range(CYP)], axis=1)
    high, low = two(lines)
    both = jnp.concatenate([high, low], axis=0)
    residue = lane_residue((256, 512))
    acc = jnp.zeros((256, 512), F32)
    for r in range(9):
        rows = slice(r * 256, (r + 1) * 256)
        block = dot(wave_hi_ref[rows, :], both) + dot(wave_lo_ref[rows, :], high)
        acc = jnp.where(residue == r, block, acc)
    high, low = two(jnp.concatenate([acc[:128], acc[128:]], axis=1))
    field = dot(high, mix_hi_ref[...], 1, 1) + dot(low, mix_hi_ref[...], 1, 1) + dot(high, mix_lo_ref[...], 1, 1)
    parts = jnp.concatenate(three(field), axis=0)
    rows = dot(slot_hots(recv_ref), parts, 1, 1)
    rows = rows[:, :128] + rows[:, 128:256] + rows[:, 256:]
    for s in range(CAP):
        out_ref[pl.ds(s, 128, stride=4), :] = rows[s * 128 : (s + 1) * 128]


def unpack_kernel(back_ref, place_ref, out_ref):
    row, col = iota((256, 256), 0), iota((256, 256), 1)
    place = jnp.broadcast_to(place_ref[...], (256, 256))
    place = jnp.sum(jnp.where(row == col, place, 0.0), axis=1, keepdims=True).astype(jnp.int32)
    hots = jnp.where(iota((256, 512), 1) == place, 1.0, 0.0).astype(BF)
    parts = jnp.concatenate(three(back_ref[...]), axis=1)
    rows = dot(hots, parts)
    out_ref[...] = rows[:, :128] + rows[:, 128:256] + rows[:, 256:]


def green_kernel(green_ref, out_ref):
    for k2 in range(16):
        turned = green_ref[:, k2, :].T
        for i in range(N_PX):
            out_ref[i, k2 * 16 : (k2 + 1) * 16, :] = turned[i * 16 : (i + 1) * 16]


def call(kernel, shape, scratch=(), dtype=F32):
    return pl.pallas_call(
        kernel,
        out_shape=jax.tree.map(lambda s: jax.ShapeDtypeStruct(s, dtype), shape, is_leaf=lambda s: isinstance(s, tuple)),
        scratch_shapes=list(scratch),
        compiler_params=PARAMS,
        name=kernel.__name__,
    )


def all_to_all(x, axes):
    return lax.all_to_all(x, axes, split_axis=0, concat_axis=0, tiled=True)


def local(charge, dest, local_ids, green_hat):
    wave, mix = z_tables()
    wave_hi, wave_lo = split_table(wave.reshape(9 * 128, 256))
    mix_hi, mix_lo = split_table(mix)
    back = wave.reshape(9, 128, 2, 128).transpose(0, 2, 3, 1).reshape(9 * 256, 128)
    back_hi, back_lo = split_table(back)
    back_hi = np.concatenate([back_hi, back_hi], axis=1)
    plane = plane_table()
    plane_hi, plane_lo = split_table(plane)
    plane_fwd = np.concatenate([plane_hi, plane_hi, plane_lo], axis=0)
    plane_back = np.concatenate([plane_hi, plane_hi], axis=1)

    turned = call(green_kernel, (8, 256, 128))(green_hat)
    green = all_to_all(turned, "px").reshape(2048, 128)

    send, place = call(pack_kernel, [(640, 128), (1, 256)])(
        charge, dest.reshape(1, 256), local_ids.reshape(1, 256)
    )
    recv = all_to_all(send.reshape(N_DEV, 5, 128), BOTH).reshape(640, 128)
    lines = call(z_forward_kernel, (512, 128))(recv, wave_hi, wave_lo, mix_hi, mix_lo)
    planes = all_to_all(lines.reshape(N_DEV, 4, 128), BOTH).reshape(512, 128)
    planes = call(
        plane_kernel,
        (512, 128),
        [pltpu.VMEM((16, 64, 128), F32), pltpu.VMEM((16, 64, 128), F32)],
    )(planes, green, plane_fwd, plane_back, plane_lo)
    lines = all_to_all(planes.reshape(N_DEV, 4, 128), BOTH).reshape(512, 128)
    rows = call(z_back_kernel, (512, 128))(lines, recv, back_hi, back_lo, mix_hi, mix_lo)
    rows = all_to_all(rows.reshape(N_DEV, 4, 128), BOTH).reshape(512, 128)
    return call(unpack_kernel, (256, 128))(rows, place)


def solution(mesh):
    return jax.shard_map(
        local,
        mesh=mesh,
        in_specs=(
            P(BOTH, None),
            P(BOTH, None),
            P(BOTH),
            P(None, "px", "pz"),
        ),
        out_specs=P(BOTH, None),
        check_vma=False,
    )
```

```python
import jax
import jax.numpy as jnp
import ml_dtypes
import numpy as np
from jax import lax
from jax.experimental import pallas as pl
from jax.experimental.pallas import tpu as pltpu
from jax.sharding import PartitionSpec as P

CXP = 8
CYP = 4
CAP = 4
N_PX = 8
N_PZ = 16
N_DEV = 128
BOTH = ("px", "pz")
RESIDUE = [0, 8] + [g for g in range(1, 8) for _ in range(2)]
BF = jnp.bfloat16
F32 = jnp.float32
VMEM = pl.BlockSpec(memory_space=pltpu.VMEM)
HBM = pl.BlockSpec(memory_space=pltpu.HBM)
PARAMS = pltpu.CompilerParams(vmem_limit_bytes=16 << 20)


def split_table(table):
    high = table.astype(np.float32).astype(ml_dtypes.bfloat16)
    low = (table - high.astype(np.float64)).astype(ml_dtypes.bfloat16)
    return high, low


def z_tables():
    device = np.arange(N_DEV)
    q = 8 * (device % N_PZ) + device // N_PZ
    l = np.arange(128)
    wave = []
    for r in range(9):
        angle = 2.0 * np.pi * ((q[:, None] * 16 + r) * l[None, :] % 2048) / 2048.0
        wave.append(np.concatenate([np.cos(angle), np.sin(angle)], axis=1))
    wave = np.stack(wave)
    mix = np.zeros((8, 4, 8, 2, 4, 16, 8))
    for c in range(8):
        for kk in range(16):
            r = RESIDUE[kk]
            angle = 2.0 * np.pi * ((r * c) % 16) / 16.0
            if kk < 2:
                cosine_part, sine_part, weight = np.cos(angle), np.cos(angle), 1.0
            elif kk % 2 == 0:
                cosine_part, sine_part, weight = np.cos(angle), -np.sin(angle), 2.0
            else:
                cosine_part, sine_part, weight = np.sin(angle), np.cos(angle), 2.0
            scale = np.sqrt(weight / 2048.0)
            for b in range(4):
                for a in range(8):
                    mix[c, b, a, 0, b, kk, a] = cosine_part * scale
                    mix[c, b, a, 1, b, kk, a] = sine_part * scale
    return wave, mix.reshape(256, 1024)


def plane_table():
    angle = 2.0 * np.pi * (np.arange(64)[:, None] * np.arange(128)[None, :] % 128) / 128.0
    return (np.cos(angle) + np.sin(angle)) / np.sqrt(128.0)


def pair_table(half):
    k = 64 * half + np.arange(64)
    cell = np.arange(64)[:, None]
    cosine = np.cos(2.0 * np.pi * (cell * k[None, :] % 128) / 128.0) * np.sqrt(2.0)
    sine = np.sin(2.0 * np.pi * (cell * k[None, :] % 128) / 128.0) * np.sqrt(2.0)
    cosine[:, 0] = np.cos(np.pi * half * np.arange(64))
    sine[:, 0] = np.cos(np.pi * (1 - half) * np.arange(64))
    return np.concatenate([cosine, sine], axis=1) / np.sqrt(128.0)


def stacked(table):
    high, low = split_table(table)
    return np.concatenate([high, high, low], axis=0), np.concatenate([high, high, low], axis=1)


def iota(shape, axis):
    return lax.broadcasted_iota(jnp.int32, shape, axis)


def two(x):
    high = x.astype(BF)
    return high, (x - high.astype(F32)).astype(BF)


def three(x):
    high = x.astype(BF)
    rest = x - high.astype(F32)
    middle = rest.astype(BF)
    return high, middle, (rest - middle.astype(F32)).astype(BF)


def dot(a, b, a_axis=1, b_axis=0):
    return lax.dot_general(a, b, (((a_axis,), (b_axis,)), ((), ())), preferred_element_type=F32)


def pack_kernel(
    charge_any, dest_any, ids_any, green_any, send_ref, place_ref, charge_ref, dest_ref, ids_ref, plane_ref, sems
):
    moves = [
        pltpu.make_async_copy(source, target, sems.at[n])
        for n, (source, target) in enumerate(
            [
                (dest_any, dest_ref),
                (ids_any, ids_ref),
                (charge_any, charge_ref),
                (green_any.at[:, 0, :], plane_ref),
            ]
        )
    ]
    for move in moves:
        move.start()
    moves[0].wait()
    dest = jnp.broadcast_to(dest_ref[...], (256, 256))
    row, col = iota((256, 256), 0), iota((256, 256), 1)
    dest_f = dest.astype(F32)
    dest_col = jnp.sum(jnp.where(row == col, dest_f, 0.0), axis=1, keepdims=True)
    earlier = (dest_col == dest_f) & (row < col)
    rank = jnp.sum(jnp.where(earlier, 1.0, 0.0), axis=0, keepdims=True)
    place_ref[...] = dest_f[0:1] * CAP + rank
    here = iota((128, 256), 0) == dest[:128]
    rank = jnp.broadcast_to(rank, (128, 256))
    moves[1].wait()
    ids = jnp.broadcast_to(ids_ref[...], (128, 256)).astype(F32)
    lane = iota((128, 128), 1)
    moves[3].wait()
    named = plane_ref[...]
    hots = []
    for slot in range(CAP):
        chosen = here & (rank == slot)
        hots.append(jnp.where(chosen, 1.0, 0.0).astype(BF))
        number = jnp.sum(jnp.where(chosen, ids + 1.0, 0.0), axis=1, keepdims=True) - 1.0
        named = jnp.where(lane == 9 + slot, number, named)
    moves[2].wait()
    parts = jnp.concatenate(three(charge_ref[...]), axis=1)
    moved = dot(jnp.concatenate(hots, axis=0), parts)
    moved = moved[:, :128] + moved[:, 128:256] + moved[:, 256:]
    for slot in range(CAP):
        send_ref[pl.ds(slot, 128, stride=5), :] = moved[slot * 128 : (slot + 1) * 128]
    send_ref[pl.ds(4, 128, stride=5), :] = named


def slot_hots(recv_ref):
    lane = iota((128, 256), 1)
    block = ((lane % 8) * 4 + (lane // 8) % 4) * 8 + lane // 32
    block = block.astype(F32)
    names = recv_ref[pl.ds(4, 128, stride=5), :]
    hots = [jnp.where(names[:, 9 + s : 10 + s] == block, 1.0, 0.0).astype(BF) for s in range(CAP)]
    return jnp.concatenate(hots, axis=0)


def lane_residue(shape):
    kk = (iota(shape, 1) // 8) % 16
    return jnp.where(kk == 0, 0, jnp.where(kk == 1, 8, kk // 2))


def z_forward_kernel(recv_ref, *refs):
    tables, out_ref, copies, sems = refs[:4], refs[4], refs[5:9], refs[9]
    moves = [pltpu.make_async_copy(tables[n], copies[n], sems.at[n]) for n in range(4)]
    for move in moves:
        move.start()
    mix_hi_ref, mix_lo_ref, wave_hi_ref, wave_lo_ref = copies
    hots = slot_hots(recv_ref)
    rows = jnp.concatenate([recv_ref[pl.ds(s, 128, stride=5), :] for s in range(CAP)], axis=0)
    parts = jnp.concatenate(three(rows), axis=1)
    field = dot(parts, hots, 0, 0)
    field = field[:128] + field[128:256] + field[256:]
    high, low = two(field)
    moves[0].wait()
    moves[1].wait()
    mixed = dot(high, mix_hi_ref[...]) + dot(low, mix_hi_ref[...]) + dot(high, mix_lo_ref[...])
    mixed = jnp.concatenate([mixed[:, :512], mixed[:, 512:]], axis=0)
    high, low = two(mixed)
    moves[2].wait()
    moves[3].wait()
    residue = lane_residue((128, 512))
    out = jnp.zeros((128, 512), F32)
    for r in range(9):
        rows = slice(r * 128, (r + 1) * 128)
        block = dot(wave_hi_ref[rows, :], high) + dot(wave_hi_ref[rows, :], low) + dot(wave_lo_ref[rows, :], high)
        out = jnp.where(residue == r, block, out)
    for b in range(CYP):
        out_ref[pl.ds(b, 128, stride=5), :] = out[:, b * 128 : (b + 1) * 128]
    ends = recv_ref[pl.ds(4, 128, stride=5), :]
    relayed = []
    for i in range(N_PX):
        source = 64 if i < 4 else 0
        rows = ends[source : source + 16]
        relayed.append(pltpu.roll(rows, 128 - 16 * i, 1) if i else rows)
    out_ref[pl.ds(4, 128, stride=5), :] = jnp.concatenate(relayed, axis=0)


def plane_kernel(spec_ref, *refs):
    pieces, refs = refs[:4], refs[4:]
    x_fwd_ref, x_back_ref, y_fwd_ref, y_back_ref, out_ref, green_ref, first_ref, second_ref, sems = refs
    me = lax.axis_index("px")
    half, place = me // 4, me % 4
    moves = []
    for n in range(4):
        source = jnp.bitwise_xor(place, n)
        start = pl.multiple_of(source * 16, 16)
        moves.append(pltpu.make_async_copy(pieces[n], green_ref.at[:, pl.ds(start, 16), :], sems.at[n]))
    for move in moves:
        move.start()
    ends = spec_ref[pl.ds(4, 128, stride=5), :].T
    y_fwd, y_back, y_low = y_fwd_ref[half], y_back_ref[half, :, :256], y_back_ref[half, :, 256:]
    x_fwd, x_back, x_low = x_fwd_ref[...], x_back_ref[:, :256], x_back_ref[:, 256:]
    for i in range(N_PX):
        rows = [spec_ref[pl.ds(i * 80 + b, 16, stride=5), :] for b in range(CYP)]
        high, low = two(jnp.concatenate(rows, axis=0))
        turned = dot(jnp.concatenate([high, low, high], axis=0), y_fwd, 0, 0)
        for kk in range(16):
            first_ref[kk, i * 8 : (i + 1) * 8, :] = turned[kk * 8 : (kk + 1) * 8]
    for move in moves:
        move.wait()
    top = iota((64, 128), 0) == 0
    for kk in range(16):
        high, low = two(first_ref[kk])
        full = dot(jnp.concatenate([high, low, high], axis=0), x_fwd, 0, 0)
        r = RESIDUE[kk]
        green = green_ref[r]
        other = jnp.where(top, ends[r : r + 1, :], green)
        full = jnp.concatenate([full[:64] * green, full[64:] * other], axis=0)
        high, low = two(full)
        second_ref[kk] = dot(x_back, jnp.concatenate([high, low], axis=1), 1, 1) + dot(x_low, high, 1, 1)
    for i in range(N_PX):
        rows = jnp.concatenate([second_ref[kk, i * 8 : (i + 1) * 8, :] for kk in range(16)], axis=0)
        high, low = two(rows)
        out_ref[i * 64 : (i + 1) * 64, :] = dot(y_back, jnp.concatenate([high, low], axis=1), 1, 1) + dot(
            y_low, high, 1, 1
        )


def z_back_kernel(spec_ref, recv_ref, wave_hi_ref, wave_lo_ref, mix_hi_ref, mix_lo_ref, out_ref):
    lines = jnp.concatenate([spec_ref[pl.ds(b, 128, stride=4), :] for b in range(CYP)], axis=1)
    high, low = two(lines)
    both = jnp.concatenate([high, low], axis=0)
    residue = lane_residue((256, 512))
    acc = jnp.zeros((256, 512), F32)
    for r in range(9):
        rows = slice(r * 256, (r + 1) * 256)
        block = dot(wave_hi_ref[rows, :], both) + dot(wave_lo_ref[rows, :], high)
        acc = jnp.where(residue == r, block, acc)
    high, low = two(jnp.concatenate([acc[:128], acc[128:]], axis=1))
    field = dot(high, mix_hi_ref[...], 1, 1) + dot(low, mix_hi_ref[...], 1, 1) + dot(high, mix_lo_ref[...], 1, 1)
    parts = jnp.concatenate(three(field), axis=0)
    rows = dot(slot_hots(recv_ref), parts, 1, 1)
    rows = rows[:, :128] + rows[:, 128:256] + rows[:, 256:]
    for s in range(CAP):
        out_ref[pl.ds(s, 128, stride=4), :] = rows[s * 128 : (s + 1) * 128]


def unpack_kernel(back_ref, place_ref, out_ref):
    row, col = iota((256, 256), 0), iota((256, 256), 1)
    place = jnp.broadcast_to(place_ref[...], (256, 256))
    place = jnp.sum(jnp.where(row == col, place, 0.0), axis=1, keepdims=True).astype(jnp.int32)
    hots = jnp.where(iota((256, 512), 1) == place, 1.0, 0.0).astype(BF)
    parts = jnp.concatenate(three(back_ref[...]), axis=1)
    rows = dot(hots, parts)
    out_ref[...] = rows[:, :128] + rows[:, 128:256] + rows[:, 256:]


def green_kernel(green_any, *refs):
    out_refs, (green_ref, turned_ref, piece_ref, sems) = refs[:4], refs[4:]
    me = lax.axis_index("px")
    move = pltpu.make_async_copy(green_any, green_ref, sems.at[0])
    move.start()
    starts = [
        pl.multiple_of((me - me % 4 + jnp.bitwise_xor(me % 4, n)) * 16, 16) for n in range(4)
    ]
    move.wait()
    for k2 in range(16):
        turned_ref[...] = green_ref[:, k2, :].T
        for n in range(4):
            piece_ref[n, pl.ds(k2, 9, stride=16), :] = turned_ref[pl.ds(starts[n], 9), :]
    moves = [pltpu.make_async_copy(piece_ref.at[n], out_refs[n], sems.at[n]) for n in range(4)]
    for move in moves:
        move.start()
    for move in moves:
        move.wait()


def call(kernel, shape, scratch=(), dtype=F32, **specs):
    return pl.pallas_call(
        kernel,
        **specs,
        out_shape=jax.tree.map(lambda s: jax.ShapeDtypeStruct(s, dtype), shape, is_leaf=lambda s: isinstance(s, tuple)),
        scratch_shapes=list(scratch),
        compiler_params=PARAMS,
        name=kernel.__name__,
    )


def all_to_all(x, axes):
    return lax.all_to_all(x, axes, split_axis=0, concat_axis=0, tiled=True)


def local(charge, dest, local_ids, green_hat):
    wave, mix = z_tables()
    wave_hi, wave_lo = split_table(wave.reshape(9 * 128, 256))
    mix_hi, mix_lo = split_table(mix)
    back = wave.reshape(9, 128, 2, 128).transpose(0, 2, 3, 1).reshape(9 * 256, 128)
    back_hi, back_lo = split_table(back)
    back_hi = np.concatenate([back_hi, back_hi], axis=1)
    x_fwd, x_back = stacked(plane_table())
    order = np.arange(64).reshape(N_PZ, CYP).T.reshape(64)
    y_fwd, y_back = (np.stack(tables) for tables in zip(stacked(pair_table(0)), stacked(pair_table(1))))
    y_fwd = y_fwd.reshape(2, 3, 64, 128)[:, :, order].reshape(2, 192, 128)

    charge, dest, local_ids, green_hat = (
        pltpu.with_memory_space_constraint(x, pltpu.HBM)
        for x in (charge, dest.reshape(1, 256), local_ids.reshape(1, 256), green_hat)
    )
    send, place = call(
        pack_kernel,
        [(640, 128), (1, 256)],
        [
            pltpu.VMEM((256, 128), F32),
            pltpu.VMEM((1, 256), jnp.int32),
            pltpu.VMEM((1, 256), jnp.int32),
            pltpu.VMEM((128, 128), F32),
            pltpu.SemaphoreType.DMA((4,)),
        ],
        in_specs=[HBM] * 4,
    )(charge, dest, local_ids, green_hat)
    recv = all_to_all(send.reshape(N_DEV, 1, 640), BOTH).reshape(640, 128)
    pieces = call(
        green_kernel,
        [(144, 128)] * 4,
        [
            pltpu.VMEM((128, 16, 128), F32),
            pltpu.VMEM((128, 128), F32),
            pltpu.VMEM((4, 144, 128), F32),
            pltpu.SemaphoreType.DMA((4,)),
        ],
        in_specs=[HBM],
        out_specs=[HBM] * 4,
    )(green_hat)
    green = [pieces[0]]
    for n in range(1, 4):
        pairs = [(i, i // 4 * 4 + ((i % 4) ^ n)) for i in range(N_PX)]
        green.append(lax.ppermute(pieces[n], "px", pairs))
    green = [
        pltpu.with_memory_space_constraint(piece.reshape(9, 16, 128), pltpu.HBM) for piece in green
    ]
    recv, green = lax.optimization_barrier((recv, green))
    tables = [pltpu.with_memory_space_constraint(jnp.asarray(x), pltpu.HBM) for x in (mix_hi, mix_lo, wave_hi, wave_lo)]
    lines = call(
        z_forward_kernel,
        (640, 128),
        [pltpu.VMEM(x.shape, BF) for x in tables] + [pltpu.SemaphoreType.DMA((4,))],
        in_specs=[VMEM] + [HBM] * 4,
    )(recv, *tables)
    planes = all_to_all(lines.reshape(N_DEV, 1, 640), BOTH).reshape(640, 128)
    planes = call(
        plane_kernel,
        (512, 128),
        [
            pltpu.VMEM((9, 64, 128), F32),
            pltpu.VMEM((16, 64, 128), F32),
            pltpu.VMEM((16, 64, 128), F32),
            pltpu.SemaphoreType.DMA((4,)),
        ],
        in_specs=[VMEM] + [HBM] * 4 + [VMEM] * 4,
    )(planes, *green, x_fwd, x_back, y_fwd, y_back)
    lines = all_to_all(planes.reshape(N_DEV, 4, 128), BOTH).reshape(512, 128)
    rows = call(z_back_kernel, (512, 128))(lines, recv, back_hi, back_lo, mix_hi, mix_lo)
    rows = all_to_all(rows.reshape(N_DEV, 4, 128), BOTH).reshape(512, 128)
    return call(unpack_kernel, (256, 128))(rows, place)


def solution(mesh):
    return jax.shard_map(
        local,
        mesh=mesh,
        in_specs=(
            P(BOTH, None),
            P(BOTH, None),
            P(BOTH),
            P(None, "px", "pz"),
        ),
        out_specs=P(BOTH, None),
        check_vma=False,
    )
```

```python
import jax
import jax.numpy as jnp
import ml_dtypes
import numpy as np
from jax import lax
from jax.experimental import pallas as pl
from jax.experimental.pallas import tpu as pltpu
from jax.sharding import PartitionSpec as P

CXP = 8
CYP = 4
CAP = 4
N_PX = 8
N_PZ = 16
N_DEV = 128
BOTH = ("px", "pz")
RESIDUE = [0, 8] + [g for g in range(1, 8) for _ in range(2)]
BF = jnp.bfloat16
F32 = jnp.float32
VMEM = pl.BlockSpec(memory_space=pltpu.VMEM)
HBM = pl.BlockSpec(memory_space=pltpu.HBM)
PARAMS = pltpu.CompilerParams(vmem_limit_bytes=16 << 20)


def split_table(table):
    high = table.astype(np.float32).astype(ml_dtypes.bfloat16)
    low = (table - high.astype(np.float64)).astype(ml_dtypes.bfloat16)
    return high, low


def z_tables():
    device = np.arange(N_DEV)
    q = 8 * (device % N_PZ) + device // N_PZ
    l = np.arange(128)
    wave = []
    for r in range(9):
        angle = 2.0 * np.pi * ((q[:, None] * 16 + r) * l[None, :] % 2048) / 2048.0
        wave.append(np.concatenate([np.cos(angle), np.sin(angle)], axis=1))
    wave = np.stack(wave)
    mix = np.zeros((8, 4, 8, 2, 4, 16, 8))
    for c in range(8):
        for kk in range(16):
            r = RESIDUE[kk]
            angle = 2.0 * np.pi * ((r * c) % 16) / 16.0
            if kk < 2:
                cosine_part, sine_part, weight = np.cos(angle), np.cos(angle), 1.0
            elif kk % 2 == 0:
                cosine_part, sine_part, weight = np.cos(angle), -np.sin(angle), 2.0
            else:
                cosine_part, sine_part, weight = np.sin(angle), np.cos(angle), 2.0
            scale = np.sqrt(weight / 2048.0)
            for b in range(4):
                for a in range(8):
                    mix[c, b, a, 0, b, kk, a] = cosine_part * scale
                    mix[c, b, a, 1, b, kk, a] = sine_part * scale
    return wave, mix.reshape(256, 1024)


def plane_table():
    angle = 2.0 * np.pi * (np.arange(64)[:, None] * np.arange(128)[None, :] % 128) / 128.0
    return (np.cos(angle) + np.sin(angle)) / np.sqrt(128.0)


def pair_table(half):
    k = 64 * half + np.arange(64)
    cell = np.arange(64)[:, None]
    cosine = np.cos(2.0 * np.pi * (cell * k[None, :] % 128) / 128.0) * np.sqrt(2.0)
    sine = np.sin(2.0 * np.pi * (cell * k[None, :] % 128) / 128.0) * np.sqrt(2.0)
    cosine[:, 0] = np.cos(np.pi * half * np.arange(64))
    sine[:, 0] = np.cos(np.pi * (1 - half) * np.arange(64))
    return np.concatenate([cosine, sine], axis=1) / np.sqrt(128.0)


def stacked(table):
    high, low = split_table(table)
    return np.concatenate([high, high, low], axis=0), np.concatenate([high, high, low], axis=1)


def iota(shape, axis):
    return lax.broadcasted_iota(jnp.int32, shape, axis)


def two(x):
    high = x.astype(BF)
    return high, (x - high.astype(F32)).astype(BF)


def three(x):
    high = x.astype(BF)
    rest = x - high.astype(F32)
    middle = rest.astype(BF)
    return high, middle, (rest - middle.astype(F32)).astype(BF)


def dot(a, b, a_axis=1, b_axis=0):
    return lax.dot_general(a, b, (((a_axis,), (b_axis,)), ((), ())), preferred_element_type=F32)


def pack_kernel(
    charge_any, dest_any, ids_any, green_any, send_ref, place_ref, charge_ref, dest_ref, ids_ref, plane_ref, sems
):
    moves = [
        pltpu.make_async_copy(source, target, sems.at[n])
        for n, (source, target) in enumerate(
            [
                (dest_any, dest_ref),
                (ids_any, ids_ref),
                (charge_any, charge_ref),
                (green_any.at[:, 0, :], plane_ref),
            ]
        )
    ]
    for move in moves:
        move.start()
    moves[0].wait()
    dest = jnp.broadcast_to(dest_ref[...], (256, 256))
    row, col = iota((256, 256), 0), iota((256, 256), 1)
    dest_f = dest.astype(F32)
    dest_col = jnp.sum(jnp.where(row == col, dest_f, 0.0), axis=1, keepdims=True)
    earlier = (dest_col == dest_f) & (row < col)
    rank = jnp.sum(jnp.where(earlier, 1.0, 0.0), axis=0, keepdims=True)
    place_ref[...] = dest_f[0:1] * CAP + rank
    here = iota((128, 256), 0) == dest[:128]
    rank = jnp.broadcast_to(rank, (128, 256))
    moves[1].wait()
    ids = jnp.broadcast_to(ids_ref[...], (128, 256)).astype(F32)
    lane = iota((128, 128), 1)
    moves[3].wait()
    named = plane_ref[...]
    hots = []
    for slot in range(CAP):
        chosen = here & (rank == slot)
        hots.append(jnp.where(chosen, 1.0, 0.0).astype(BF))
        number = jnp.sum(jnp.where(chosen, ids + 1.0, 0.0), axis=1, keepdims=True) - 1.0
        named = jnp.where(lane == 9 + slot, number, named)
    moves[2].wait()
    parts = jnp.concatenate(three(charge_ref[...]), axis=1)
    moved = dot(jnp.concatenate(hots, axis=0), parts)
    moved = moved[:, :128] + moved[:, 128:256] + moved[:, 256:]
    for slot in range(CAP):
        send_ref[pl.ds(slot, 128, stride=5), :] = moved[slot * 128 : (slot + 1) * 128]
    send_ref[pl.ds(4, 128, stride=5), :] = named


def block_name(index):
    return (((index % 8) * 4 + (index // 8) % 4) * 8 + index // 32).astype(F32)


def slot_rows(r):
    first, count = (0, 8) if r == 0 else (8, 8) if r == 8 else (16 * r, 16)
    return [slice(b * 128 + first, b * 128 + first + count) for b in range(CYP)], count


def z_forward_kernel(recv_ref, mix_ref, wave_ref, out_ref, turned_ref):
    ends = recv_ref[pl.ds(4, 128, stride=5), :]
    names = ends.T
    block = block_name(iota((256, 128), 0))
    hots = [jnp.where(block == names[9 + s : 10 + s, :], 1.0, 0.0).astype(BF) for s in range(CAP)]
    rows = jnp.concatenate([recv_ref[pl.ds(s, 128, stride=5), :] for s in range(CAP)], axis=0)
    field = dot(jnp.concatenate(hots, axis=1), jnp.concatenate(three(rows), axis=1))
    field = field[:, :128] + field[:, 128:256] + field[:, 256:]
    high, low = two(field)
    mixed = dot(mix_ref[:1024], jnp.concatenate([high, low], axis=1))
    mixed = mixed[:, :128] + mixed[:, 128:] + dot(mix_ref[1024:], high)
    mixed = jnp.concatenate([mixed[:512], mixed[512:]], axis=1)
    for r in range(9):
        places, count = slot_rows(r)
        high, low = two(jnp.concatenate([mixed[place] for place in places], axis=0))
        block = dot(jnp.concatenate([high, low], axis=0), wave_ref[r * 256 : (r + 1) * 256, :])
        size = 4 * count
        block = block[:size, :128] + block[:size, 128:] + block[size:, :128]
        for b, place in enumerate(places):
            turned_ref[place, :] = block[b * count : (b + 1) * count]
    for b in range(CYP):
        out_ref[pl.ds(b, 128, stride=5), :] = turned_ref[b * 128 : (b + 1) * 128, :].T
    relayed = []
    for i in range(N_PX):
        source = 64 if i < 4 else 0
        rows = ends[source : source + 16]
        relayed.append(pltpu.roll(rows, 128 - 16 * i, 1) if i else rows)
    out_ref[pl.ds(4, 128, stride=5), :] = jnp.concatenate(relayed, axis=0)


def plane_kernel(spec_ref, *refs):
    pieces, refs = refs[:4], refs[4:]
    x_fwd_ref, x_back_ref, y_fwd_ref, y_back_ref, out_ref, green_ref, first_ref, second_ref = refs
    me = lax.axis_index("px")
    half, place = me // 4, me % 4
    for n in range(4):
        start = pl.multiple_of(jnp.bitwise_xor(place, n) * 16, 16)
        for r in range(9):
            green_ref[r, pl.ds(start, 16), :] = pieces[n][r * 16 : (r + 1) * 16, :]
    ends = spec_ref[pl.ds(4, 128, stride=5), :].T
    y_fwd, y_back, y_low = y_fwd_ref[half], y_back_ref[half, :, :256], y_back_ref[half, :, 256:]
    x_fwd, x_back, x_low = x_fwd_ref[...], x_back_ref[:, :256], x_back_ref[:, 256:]
    for i in range(N_PX):
        rows = [spec_ref[pl.ds(i * 80 + b, 16, stride=5), :] for b in range(CYP)]
        high, low = two(jnp.concatenate(rows, axis=0))
        turned = dot(jnp.concatenate([high, low, high], axis=0), y_fwd, 0, 0)
        for kk in range(16):
            first_ref[kk, i * 8 : (i + 1) * 8, :] = turned[kk * 8 : (kk + 1) * 8]
    top = iota((64, 128), 0) == 0
    for kk in range(16):
        high, low = two(first_ref[kk])
        full = dot(jnp.concatenate([high, low, high], axis=0), x_fwd, 0, 0)
        r = RESIDUE[kk]
        green = green_ref[r]
        other = jnp.where(top, ends[r : r + 1, :], green)
        full = jnp.concatenate([full[:64] * green, full[64:] * other], axis=0)
        high, low = two(full)
        second_ref[kk] = dot(x_back, jnp.concatenate([high, low], axis=1), 1, 1) + dot(x_low, high, 1, 1)
    for i in range(N_PX):
        rows = jnp.concatenate([second_ref[kk, i * 8 : (i + 1) * 8, :] for kk in range(16)], axis=0)
        high, low = two(rows)
        out_ref[i * 64 : (i + 1) * 64, :] = dot(y_back, jnp.concatenate([high, low], axis=1), 1, 1) + dot(
            y_low, high, 1, 1
        )


def z_back_kernel(spec_ref, recv_ref, wave_hi_ref, wave_lo_ref, mix_hi_ref, mix_lo_ref, out_ref, turned_ref, line_ref):
    for b in range(CYP):
        turned_ref[b * 128 : (b + 1) * 128, :] = spec_ref[pl.ds(b, 128, stride=4), :].T
    for r in range(9):
        places, count = slot_rows(r)
        high, low = two(jnp.concatenate([turned_ref[place, :] for place in places], axis=0))
        rows = slice(r * 128, (r + 1) * 128)
        size = 4 * count
        block = dot(jnp.concatenate([high, low], axis=0), wave_hi_ref[rows, :])
        block = block[:size] + block[size:] + dot(high, wave_lo_ref[rows, :])
        for b, place in enumerate(places):
            part = block[b * count : (b + 1) * count]
            line_ref[place, :] = part[:, :128]
            line_ref[slice(place.start + 512, place.stop + 512), :] = part[:, 128:]
    high, low = two(line_ref[...])
    field = dot(mix_hi_ref[...], jnp.concatenate([high, low], axis=1))
    field = field[:, :128] + field[:, 128:] + dot(mix_lo_ref[...], high)
    block = block_name(iota((128, 256), 1))
    names = recv_ref[pl.ds(4, 128, stride=5), :]
    hots = [jnp.where(names[:, 9 + s : 10 + s] == block, 1.0, 0.0).astype(BF) for s in range(CAP)]
    rows = dot(jnp.concatenate(hots, axis=0), jnp.concatenate(three(field), axis=1))
    rows = rows[:, :128] + rows[:, 128:256] + rows[:, 256:]
    for s in range(CAP):
        out_ref[pl.ds(s, 128, stride=4), :] = rows[s * 128 : (s + 1) * 128]


def unpack_kernel(back_ref, place_ref, out_ref):
    row, col = iota((256, 256), 0), iota((256, 256), 1)
    place = jnp.broadcast_to(place_ref[...], (256, 256))
    place = jnp.sum(jnp.where(row == col, place, 0.0), axis=1, keepdims=True).astype(jnp.int32)
    hots = jnp.where(iota((256, 512), 1) == place, 1.0, 0.0).astype(BF)
    parts = jnp.concatenate(three(back_ref[...]), axis=1)
    rows = dot(hots, parts)
    out_ref[...] = rows[:, :128] + rows[:, 128:256] + rows[:, 256:]


def green_kernel(green_any, *refs):
    tables, out_refs, copies, (green_ref, turned_ref, piece_ref, sems) = refs[:6], refs[6:10], refs[10:16], refs[16:]
    me = lax.axis_index("px")
    moves = [pltpu.make_async_copy(green_any, green_ref, sems.at[0])]
    for n in range(6):
        moves.append(pltpu.make_async_copy(tables[n], copies[n], sems.at[n + 1]))
    for move in moves:
        move.start()
    starts = [
        pl.multiple_of((me - me % 4 + jnp.bitwise_xor(me % 4, n)) * 16, 16) for n in range(4)
    ]
    moves[0].wait()
    for k2 in range(16):
        turned_ref[...] = green_ref[:, k2, :].T
        for n in range(4):
            piece_ref[n, pl.ds(k2, 9, stride=16), :] = turned_ref[pl.ds(starts[n], 9), :]
    stores = [pltpu.make_async_copy(piece_ref.at[n], out_refs[n], sems.at[n + 7]) for n in range(4)]
    for move in stores:
        move.start()
    for move in moves[1:] + stores:
        move.wait()


def call(kernel, shape, scratch=(), dtype=F32, **specs):
    return pl.pallas_call(
        kernel,
        **specs,
        out_shape=jax.tree.map(
            lambda s: jax.ShapeDtypeStruct(s, dtype) if isinstance(s, tuple) else s,
            shape,
            is_leaf=lambda s: isinstance(s, tuple),
        ),
        scratch_shapes=list(scratch),
        compiler_params=PARAMS,
        name=kernel.__name__,
    )


def all_to_all(x, axes):
    return lax.all_to_all(x, axes, split_axis=0, concat_axis=0, tiled=True)


def local(charge, dest, local_ids, green_hat):
    wave, mix = z_tables()
    mix_hi, mix_lo = split_table(mix)
    mix_both = np.concatenate([mix_hi.T, mix_lo.T], axis=0)
    wave_hi, wave_lo = split_table(wave.reshape(9 * 128, 256))
    wave_both = np.concatenate(split_table(wave.transpose(0, 2, 1).reshape(9 * 256, 128)), axis=1)
    x_fwd, x_back = stacked(plane_table())
    order = np.arange(64).reshape(N_PZ, CYP).T.reshape(64)
    y_fwd, y_back = (np.stack(tables) for tables in zip(stacked(pair_table(0)), stacked(pair_table(1))))
    y_fwd = y_fwd.reshape(2, 3, 64, 128)[:, :, order].reshape(2, 192, 128)

    charge, dest, local_ids, green_hat = (
        pltpu.with_memory_space_constraint(x, pltpu.HBM)
        for x in (charge, dest.reshape(1, 256), local_ids.reshape(1, 256), green_hat)
    )
    send, place = call(
        pack_kernel,
        [(640, 128), (1, 256)],
        [
            pltpu.VMEM((256, 128), F32),
            pltpu.VMEM((1, 256), jnp.int32),
            pltpu.VMEM((1, 256), jnp.int32),
            pltpu.VMEM((128, 128), F32),
            pltpu.SemaphoreType.DMA((4,)),
        ],
        in_specs=[HBM] * 4,
    )(charge, dest, local_ids, green_hat)
    recv = all_to_all(send.reshape(N_DEV, 1, 640), BOTH).reshape(640, 128)
    tables = [
        pltpu.with_memory_space_constraint(jnp.asarray(x), pltpu.HBM)
        for x in (mix_both, wave_both, x_fwd, x_back, y_fwd, y_back)
    ]
    *pieces, mix_both, wave_both, x_fwd, x_back, y_fwd, y_back = call(
        green_kernel,
        [pltpu.HBM((144, 128), F32)] * 4 + [jax.ShapeDtypeStruct(x.shape, BF) for x in tables],
        [
            pltpu.VMEM((128, 16, 128), F32),
            pltpu.VMEM((128, 128), F32),
            pltpu.VMEM((4, 144, 128), F32),
            pltpu.SemaphoreType.DMA((11,)),
        ],
        in_specs=[HBM] * 7,
        out_specs=[HBM] * 4 + [VMEM] * 6,
    )(green_hat, *tables)
    green = [pieces[0]]
    for n in range(1, 4):
        pairs = [(i, i // 4 * 4 + ((i % 4) ^ n)) for i in range(N_PX)]
        green.append(lax.ppermute(pieces[n], "px", pairs))
    lines = call(z_forward_kernel, (640, 128), [pltpu.VMEM((512, 128), F32)])(recv, mix_both, wave_both)
    planes = all_to_all(lines.reshape(N_DEV, 1, 640), BOTH).reshape(640, 128)
    planes = call(
        plane_kernel,
        (512, 128),
        [
            pltpu.VMEM((9, 64, 128), F32),
            pltpu.VMEM((16, 64, 128), F32),
            pltpu.VMEM((16, 64, 128), F32),
        ],
    )(planes, *green, x_fwd, x_back, y_fwd, y_back)
    lines = all_to_all(planes.reshape(N_DEV, 4, 128), BOTH).reshape(512, 128)
    rows = call(z_back_kernel, (512, 128), [pltpu.VMEM((512, 128), F32), pltpu.VMEM((1024, 128), F32)])(
        lines, recv, wave_hi, wave_lo, mix_hi, mix_lo
    )
    rows = all_to_all(rows.reshape(N_DEV, 4, 128), BOTH).reshape(512, 128)
    return call(unpack_kernel, (256, 128))(rows, place)


def solution(mesh):
    return jax.shard_map(
        local,
        mesh=mesh,
        in_specs=(
            P(BOTH, None),
            P(BOTH, None),
            P(BOTH),
            P(None, "px", "pz"),
        ),
        out_specs=P(BOTH, None),
        check_vma=False,
    )
```

```python
import jax
import jax.numpy as jnp
import ml_dtypes
import numpy as np
from jax import lax
from jax.experimental import pallas as pl
from jax.experimental.pallas import tpu as pltpu
from jax.sharding import PartitionSpec as P

CXP = 8
CYP = 4
CAP = 4
N_PX = 8
N_PZ = 16
N_DEV = 128
BOTH = ("px", "pz")
RESIDUE = [0, 8] + [g for g in range(1, 8) for _ in range(2)]
BF = jnp.bfloat16
F32 = jnp.float32
VMEM = pl.BlockSpec(memory_space=pltpu.VMEM)
HBM = pl.BlockSpec(memory_space=pltpu.HBM)
PARAMS = pltpu.CompilerParams(vmem_limit_bytes=16 << 20)


def split_table(table):
    high = table.astype(np.float32).astype(ml_dtypes.bfloat16)
    low = (table - high.astype(np.float64)).astype(ml_dtypes.bfloat16)
    return high, low


def z_tables():
    device = np.arange(N_DEV)
    q = 8 * (device % N_PZ) + device // N_PZ
    l = np.arange(128)
    wave = []
    for r in range(9):
        angle = 2.0 * np.pi * ((q[:, None] * 16 + r) * l[None, :] % 2048) / 2048.0
        wave.append(np.concatenate([np.cos(angle), np.sin(angle)], axis=1))
    wave = np.stack(wave)
    mix = np.zeros((8, 4, 8, 2, 4, 16, 8))
    for c in range(8):
        for kk in range(16):
            r = RESIDUE[kk]
            angle = 2.0 * np.pi * ((r * c) % 16) / 16.0
            if kk < 2:
                cosine_part, sine_part, weight = np.cos(angle), np.cos(angle), 1.0
            elif kk % 2 == 0:
                cosine_part, sine_part, weight = np.cos(angle), -np.sin(angle), 2.0
            else:
                cosine_part, sine_part, weight = np.sin(angle), np.cos(angle), 2.0
            scale = np.sqrt(weight / 2048.0)
            for b in range(4):
                for a in range(8):
                    mix[c, b, a, 0, b, kk, a] = cosine_part * scale
                    mix[c, b, a, 1, b, kk, a] = sine_part * scale
    return wave, mix.reshape(256, 1024)


def pair_table(half):
    k = 64 * half + np.arange(64)
    cell = np.arange(64)[:, None]
    cosine = np.cos(2.0 * np.pi * (cell * k[None, :] % 128) / 128.0) * np.sqrt(2.0)
    sine = np.sin(2.0 * np.pi * (cell * k[None, :] % 128) / 128.0) * np.sqrt(2.0)
    cosine[:, 0] = np.cos(np.pi * half * np.arange(64))
    sine[:, 0] = np.cos(np.pi * (1 - half) * np.arange(64))
    return np.concatenate([cosine, sine], axis=1) / np.sqrt(128.0)


def stacked(table):
    high, low = split_table(table)
    return np.concatenate([high, high, low], axis=0), np.concatenate([high, high, low], axis=1)


def iota(shape, axis):
    return lax.broadcasted_iota(jnp.int32, shape, axis)


def two(x):
    high = x.astype(BF)
    return high, (x - high.astype(F32)).astype(BF)


def three(x):
    high = x.astype(BF)
    rest = x - high.astype(F32)
    middle = rest.astype(BF)
    return high, middle, (rest - middle.astype(F32)).astype(BF)


def dot(a, b, a_axis=1, b_axis=0):
    return lax.dot_general(a, b, (((a_axis,), (b_axis,)), ((), ())), preferred_element_type=F32)


def pack_kernel(
    charge_any, dest_any, ids_any, green_any, send_ref, place_ref, charge_ref, dest_ref, ids_ref, plane_ref, sems
):
    moves = [
        pltpu.make_async_copy(source, target, sems.at[n])
        for n, (source, target) in enumerate(
            [
                (dest_any, dest_ref),
                (ids_any, ids_ref),
                (charge_any, charge_ref),
                (green_any.at[:, 0, :], plane_ref),
            ]
        )
    ]
    for move in moves:
        move.start()
    moves[0].wait()
    dest = jnp.broadcast_to(dest_ref[...], (256, 256))
    row, col = iota((256, 256), 0), iota((256, 256), 1)
    dest_f = dest.astype(F32)
    dest_col = jnp.sum(jnp.where(row == col, dest_f, 0.0), axis=1, keepdims=True)
    earlier = (dest_col == dest_f) & (row < col)
    rank = jnp.sum(jnp.where(earlier, 1.0, 0.0), axis=0, keepdims=True)
    place_ref[...] = dest_f[0:1] * CAP + rank
    here = iota((128, 256), 0) == dest[:128]
    rank = jnp.broadcast_to(rank, (128, 256))
    moves[1].wait()
    ids = jnp.broadcast_to(ids_ref[...], (128, 256)).astype(F32)
    lane = iota((128, 128), 1)
    moves[3].wait()
    named = plane_ref[...]
    hots = []
    for slot in range(CAP):
        chosen = here & (rank == slot)
        hots.append(jnp.where(chosen, 1.0, 0.0).astype(BF))
        number = jnp.sum(jnp.where(chosen, ids + 1.0, 0.0), axis=1, keepdims=True) - 1.0
        named = jnp.where(lane == 9 + slot, number, named)
    moves[2].wait()
    parts = jnp.concatenate(three(charge_ref[...]), axis=1)
    moved = dot(jnp.concatenate(hots, axis=0), parts)
    moved = moved[:, :128] + moved[:, 128:256] + moved[:, 256:]
    for slot in range(CAP):
        send_ref[pl.ds(slot, 128, stride=5), :] = moved[slot * 128 : (slot + 1) * 128]
    send_ref[pl.ds(4, 128, stride=5), :] = named


def block_name(index):
    return (((index % 8) * 4 + (index // 8) % 4) * 8 + index // 32).astype(F32)


def slot_rows(r):
    first, count = (0, 8) if r == 0 else (8, 8) if r == 8 else (16 * r, 16)
    return [slice(b * 128 + first, b * 128 + first + count) for b in range(CYP)], count


def z_forward_kernel(recv_ref, mix_ref, wave_ref, out_ref, turned_ref):
    ends = recv_ref[pl.ds(4, 128, stride=5), :]
    names = ends.T
    block = block_name(iota((256, 128), 0))
    hots = [jnp.where(block == names[9 + s : 10 + s, :], 1.0, 0.0).astype(BF) for s in range(CAP)]
    rows = jnp.concatenate([recv_ref[pl.ds(s, 128, stride=5), :] for s in range(CAP)], axis=0)
    field = dot(jnp.concatenate(hots, axis=1), jnp.concatenate(three(rows), axis=1))
    field = field[:, :128] + field[:, 128:256] + field[:, 256:]
    high, low = two(field)
    mixed = dot(mix_ref[:1024], jnp.concatenate([high, low], axis=1))
    mixed = mixed[:, :128] + mixed[:, 128:] + dot(mix_ref[1024:], high)
    mixed = jnp.concatenate([mixed[:512], mixed[512:]], axis=1)
    for r in range(9):
        places, count = slot_rows(r)
        high, low = two(jnp.concatenate([mixed[place] for place in places], axis=0))
        block = dot(jnp.concatenate([high, low], axis=0), wave_ref[r * 256 : (r + 1) * 256, :])
        size = 4 * count
        block = block[:size, :128] + block[:size, 128:] + block[size:, :128]
        for b, place in enumerate(places):
            turned_ref[place, :] = block[b * count : (b + 1) * count]
    for b in range(CYP):
        out_ref[pl.ds(b, 128, stride=5), :] = turned_ref[b * 128 : (b + 1) * 128, :].T
    relayed = []
    for i in range(N_PX):
        source = 64 if i < 4 else 0
        rows = ends[source : source + 16]
        relayed.append(pltpu.roll(rows, 128 - 16 * i, 1) if i else rows)
    out_ref[pl.ds(4, 128, stride=5), :] = jnp.concatenate(relayed, axis=0)


def plane_kernel(spec_ref, *refs):
    pieces, refs = refs[:4], refs[4:]
    x_fwd_ref, x_back_ref, y_fwd_ref, y_back_ref, out_ref, green_ref, first_ref, second_ref = refs
    me = lax.axis_index("px")
    half, place = me // 4, me % 4
    left, middle = iota((16, 128), 1) < 64, iota((16, 128), 1) == 64
    for n in range(4):
        start = pl.multiple_of(jnp.bitwise_xor(place, n) * 16, 16)
        last = pieces[n][64:80, :]
        for r in range(9):
            pair = pieces[n][r // 2 * 16 : (r // 2 + 1) * 16, :]
            swapped = pltpu.roll(pair, 64, 1)
            both = jnp.where(left, swapped, pair) if r % 2 else jnp.where(left, pair, swapped)
            both = jnp.where(middle, last[:, 64 + r : 65 + r], both)
            green_ref[r, pl.ds(start, 16), :] = both
    ends = spec_ref[pl.ds(4, 128, stride=5), :].T[:16]
    ends = jnp.where(left | middle, ends, pltpu.roll(ends, 64, 1))
    y_fwd, y_back, y_low = y_fwd_ref[half], y_back_ref[half, :, :256], y_back_ref[half, :, 256:]
    x_fwd, x_back, x_low = x_fwd_ref[...], x_back_ref[:, :256], x_back_ref[:, 256:]
    for i in range(N_PX):
        rows = [spec_ref[pl.ds(i * 80 + b, 16, stride=5), :] for b in range(CYP)]
        high, low = two(jnp.concatenate(rows, axis=0))
        turned = dot(jnp.concatenate([high, low, high], axis=0), y_fwd, 0, 0)
        for kk in range(16):
            first_ref[kk, i * 8 : (i + 1) * 8, :] = turned[kk * 8 : (kk + 1) * 8]
    top = iota((64, 128), 0) == 0
    for kk in range(16):
        high, low = two(first_ref[kk])
        full = dot(jnp.concatenate([high, low, high], axis=0), x_fwd, 0, 0)
        r = RESIDUE[kk]
        green = green_ref[r]
        other = jnp.where(top, ends[r : r + 1, :], green)
        full = jnp.concatenate([full[:64] * green, full[64:] * other], axis=0)
        high, low = two(full)
        second_ref[kk] = dot(x_back, jnp.concatenate([high, low], axis=1), 1, 1) + dot(x_low, high, 1, 1)
    for i in range(N_PX):
        rows = jnp.concatenate([second_ref[kk, i * 8 : (i + 1) * 8, :] for kk in range(16)], axis=0)
        high, low = two(rows)
        out_ref[i * 64 : (i + 1) * 64, :] = dot(y_back, jnp.concatenate([high, low], axis=1), 1, 1) + dot(
            y_low, high, 1, 1
        )


def z_back_kernel(spec_ref, recv_ref, wave_hi_ref, wave_lo_ref, mix_hi_ref, mix_lo_ref, out_ref, turned_ref, line_ref):
    for b in range(CYP):
        turned_ref[b * 128 : (b + 1) * 128, :] = spec_ref[pl.ds(b, 128, stride=4), :].T
    for r in range(9):
        places, count = slot_rows(r)
        high, low = two(jnp.concatenate([turned_ref[place, :] for place in places], axis=0))
        rows = slice(r * 128, (r + 1) * 128)
        size = 4 * count
        block = dot(jnp.concatenate([high, low], axis=0), wave_hi_ref[rows, :])
        block = block[:size] + block[size:] + dot(high, wave_lo_ref[rows, :])
        for b, place in enumerate(places):
            part = block[b * count : (b + 1) * count]
            line_ref[place, :] = part[:, :128]
            line_ref[slice(place.start + 512, place.stop + 512), :] = part[:, 128:]
    high, low = two(line_ref[...])
    field = dot(mix_hi_ref[...], jnp.concatenate([high, low], axis=1))
    field = field[:, :128] + field[:, 128:] + dot(mix_lo_ref[...], high)
    block = block_name(iota((128, 256), 1))
    names = recv_ref[pl.ds(4, 128, stride=5), :]
    hots = [jnp.where(names[:, 9 + s : 10 + s] == block, 1.0, 0.0).astype(BF) for s in range(CAP)]
    rows = dot(jnp.concatenate(hots, axis=0), jnp.concatenate(three(field), axis=1))
    rows = rows[:, :128] + rows[:, 128:256] + rows[:, 256:]
    for s in range(CAP):
        out_ref[pl.ds(s, 128, stride=4), :] = rows[s * 128 : (s + 1) * 128]


def unpack_kernel(back_ref, place_ref, out_ref):
    row, col = iota((256, 256), 0), iota((256, 256), 1)
    place = jnp.broadcast_to(place_ref[...], (256, 256))
    place = jnp.sum(jnp.where(row == col, place, 0.0), axis=1, keepdims=True).astype(jnp.int32)
    hots = jnp.where(iota((256, 512), 1) == place, 1.0, 0.0).astype(BF)
    parts = jnp.concatenate(three(back_ref[...]), axis=1)
    rows = dot(hots, parts)
    out_ref[...] = rows[:, :128] + rows[:, 128:256] + rows[:, 256:]


def green_kernel(green_any, *refs):
    tables, out_refs, copies, (green_ref, turned_ref, piece_ref, sems) = refs[:6], refs[6:10], refs[10:16], refs[16:]
    me = lax.axis_index("px")
    moves = [pltpu.make_async_copy(green_any, green_ref, sems.at[0])]
    for n in range(6):
        moves.append(pltpu.make_async_copy(tables[n], copies[n], sems.at[n + 1]))
    for move in moves:
        move.start()
    starts = [
        pl.multiple_of((me - me % 4 + jnp.bitwise_xor(me % 4, n)) * 16, 16) for n in range(4)
    ]
    left = iota((16, 128), 1) < 64
    moves[0].wait()
    for k2 in range(16):
        turned_ref[...] = green_ref[:, k2, :].T
        for n in range(4):
            even = turned_ref[pl.ds(starts[n], 4, stride=2), :]
            odd = pltpu.roll(turned_ref[pl.ds(starts[n] + 1, 4, stride=2), :], 64, 1)
            piece_ref[n, pl.ds(k2, 4, stride=16), :] = jnp.where(left[:4], even, odd)
            piece_ref[n, pl.ds(k2 + 64, 1), :] = turned_ref[pl.ds(starts[n] + 8, 1), :]
    for n in range(4):
        ends = pltpu.roll(green_ref[64], 192 - starts[n], 1)
        piece_ref[n, 64:80, :] = jnp.where(left, piece_ref[n, 64:80, :], ends)
    stores = [pltpu.make_async_copy(piece_ref.at[n], out_refs[n], sems.at[n + 7]) for n in range(4)]
    for move in stores:
        move.start()
    for move in moves[1:] + stores:
        move.wait()


def call(kernel, shape, scratch=(), dtype=F32, **specs):
    return pl.pallas_call(
        kernel,
        **specs,
        out_shape=jax.tree.map(
            lambda s: jax.ShapeDtypeStruct(s, dtype) if isinstance(s, tuple) else s,
            shape,
            is_leaf=lambda s: isinstance(s, tuple),
        ),
        scratch_shapes=list(scratch),
        compiler_params=PARAMS,
        name=kernel.__name__,
    )


def all_to_all(x, axes):
    return lax.all_to_all(x, axes, split_axis=0, concat_axis=0, tiled=True)


def local(charge, dest, local_ids, green_hat):
    wave, mix = z_tables()
    mix_hi, mix_lo = split_table(mix)
    mix_both = np.concatenate([mix_hi.T, mix_lo.T], axis=0)
    wave_hi, wave_lo = split_table(wave.reshape(9 * 128, 256))
    wave_both = np.concatenate(split_table(wave.transpose(0, 2, 1).reshape(9 * 256, 128)), axis=1)
    x_fwd, x_back = stacked(pair_table(0))
    order = np.arange(64).reshape(N_PZ, CYP).T.reshape(64)
    y_fwd, y_back = (np.stack(tables) for tables in zip(stacked(pair_table(0)), stacked(pair_table(1))))
    y_fwd = y_fwd.reshape(2, 3, 64, 128)[:, :, order].reshape(2, 192, 128)

    charge, dest, local_ids, green_hat = (
        pltpu.with_memory_space_constraint(x, pltpu.HBM)
        for x in (charge, dest.reshape(1, 256), local_ids.reshape(1, 256), green_hat)
    )
    send, place = call(
        pack_kernel,
        [(640, 128), (1, 256)],
        [
            pltpu.VMEM((256, 128), F32),
            pltpu.VMEM((1, 256), jnp.int32),
            pltpu.VMEM((1, 256), jnp.int32),
            pltpu.VMEM((128, 128), F32),
            pltpu.SemaphoreType.DMA((4,)),
        ],
        in_specs=[HBM] * 4,
    )(charge, dest, local_ids, green_hat)
    recv = all_to_all(send.reshape(N_DEV, 1, 640), BOTH).reshape(640, 128)
    tables = [
        pltpu.with_memory_space_constraint(jnp.asarray(x), pltpu.HBM)
        for x in (mix_both, wave_both, x_fwd, x_back, y_fwd, y_back)
    ]
    *pieces, mix_both, wave_both, x_fwd, x_back, y_fwd, y_back = call(
        green_kernel,
        [pltpu.HBM((80, 128), F32)] * 4 + [jax.ShapeDtypeStruct(x.shape, BF) for x in tables],
        [
            pltpu.VMEM((128, 16, 128), F32),
            pltpu.VMEM((128, 128), F32),
            pltpu.VMEM((4, 80, 128), F32),
            pltpu.SemaphoreType.DMA((11,)),
        ],
        in_specs=[HBM] * 7,
        out_specs=[HBM] * 4 + [VMEM] * 6,
    )(green_hat, *tables)
    green = [pieces[0]]
    for n in range(1, 4):
        pairs = [(i, i // 4 * 4 + ((i % 4) ^ n)) for i in range(N_PX)]
        green.append(lax.ppermute(pieces[n], "px", pairs))
    lines = call(z_forward_kernel, (640, 128), [pltpu.VMEM((512, 128), F32)])(recv, mix_both, wave_both)
    planes = all_to_all(lines.reshape(N_DEV, 1, 640), BOTH).reshape(640, 128)
    planes = call(
        plane_kernel,
        (512, 128),
        [
            pltpu.VMEM((9, 64, 128), F32),
            pltpu.VMEM((16, 64, 128), F32),
            pltpu.VMEM((16, 64, 128), F32),
        ],
    )(planes, *green, x_fwd, x_back, y_fwd, y_back)
    lines = all_to_all(planes.reshape(N_DEV, 4, 128), BOTH).reshape(512, 128)
    rows = call(z_back_kernel, (512, 128), [pltpu.VMEM((512, 128), F32), pltpu.VMEM((1024, 128), F32)])(
        lines, recv, wave_hi, wave_lo, mix_hi, mix_lo
    )
    rows = all_to_all(rows.reshape(N_DEV, 4, 128), BOTH).reshape(512, 128)
    return call(unpack_kernel, (256, 128))(rows, place)


def solution(mesh):
    return jax.shard_map(
        local,
        mesh=mesh,
        in_specs=(
            P(BOTH, None),
            P(BOTH, None),
            P(BOTH),
            P(None, "px", "pz"),
        ),
        out_specs=P(BOTH, None),
        check_vma=False,
    )
```

```python
import jax
import jax.numpy as jnp
import ml_dtypes
import numpy as np
from jax import lax
from jax.experimental import pallas as pl
from jax.experimental.pallas import tpu as pltpu
from jax.sharding import PartitionSpec as P

CXP = 8
CYP = 4
CAP = 4
N_PX = 8
N_PZ = 16
N_DEV = 128
BOTH = ("px", "pz")
RESIDUE = [0, 8] + [g for g in range(1, 8) for _ in range(2)]
BF = jnp.bfloat16
F32 = jnp.float32
VMEM = pl.BlockSpec(memory_space=pltpu.VMEM)
HBM = pl.BlockSpec(memory_space=pltpu.HBM)
PARAMS = pltpu.CompilerParams(vmem_limit_bytes=16 << 20)


def split_table(table):
    high = table.astype(np.float32).astype(ml_dtypes.bfloat16)
    low = (table - high.astype(np.float64)).astype(ml_dtypes.bfloat16)
    return high, low


def z_tables():
    device = np.arange(N_DEV)
    q = 8 * (device % N_PZ) + device // N_PZ
    l = np.arange(128)
    wave = []
    for r in range(9):
        angle = 2.0 * np.pi * ((q[:, None] * 16 + r) * l[None, :] % 2048) / 2048.0
        wave.append(np.concatenate([np.cos(angle), np.sin(angle)], axis=1))
    wave = np.stack(wave)
    mix = np.zeros((8, 4, 8, 2, 4, 16, 8))
    for c in range(8):
        for kk in range(16):
            r = RESIDUE[kk]
            angle = 2.0 * np.pi * ((r * c) % 16) / 16.0
            if kk < 2:
                cosine_part, sine_part, weight = np.cos(angle), np.cos(angle), 1.0
            elif kk % 2 == 0:
                cosine_part, sine_part, weight = np.cos(angle), -np.sin(angle), 2.0
            else:
                cosine_part, sine_part, weight = np.sin(angle), np.cos(angle), 2.0
            scale = np.sqrt(weight / 2048.0)
            for b in range(4):
                for a in range(8):
                    mix[c, b, a, 0, b, kk, a] = cosine_part * scale
                    mix[c, b, a, 1, b, kk, a] = sine_part * scale
    return wave, mix.reshape(256, 1024)


def pair_table(half):
    k = 64 * half + np.arange(64)
    cell = np.arange(64)[:, None]
    cosine = np.cos(2.0 * np.pi * (cell * k[None, :] % 128) / 128.0) * np.sqrt(2.0)
    sine = np.sin(2.0 * np.pi * (cell * k[None, :] % 128) / 128.0) * np.sqrt(2.0)
    cosine[:, 0] = np.cos(np.pi * half * np.arange(64))
    sine[:, 0] = np.cos(np.pi * (1 - half) * np.arange(64))
    return np.concatenate([cosine, sine], axis=1) / np.sqrt(128.0)


def stacked(table):
    high, low = split_table(table)
    none = np.zeros_like(low)
    fwd = np.block([[high, low], [high, none]])
    back = np.block([[high.T, low.T], [high.T, none.T]])
    return fwd, back


def iota(shape, axis):
    return lax.broadcasted_iota(jnp.int32, shape, axis)


def two(x):
    high = x.astype(BF)
    return high, (x - high.astype(F32)).astype(BF)


def three(x):
    high = x.astype(BF)
    rest = x - high.astype(F32)
    middle = rest.astype(BF)
    return high, middle, (rest - middle.astype(F32)).astype(BF)


def turned_pair(x):
    high = x.astype(BF).astype(F32)
    return jnp.concatenate([high, x - high], axis=0).T.astype(BF)


def halves(x, size):
    return x[:, :size] + x[:, size:]


def dot(a, b, a_axis=1, b_axis=0):
    return lax.dot_general(a, b, (((a_axis,), (b_axis,)), ((), ())), preferred_element_type=F32)


def pack_kernel(
    charge_any, dest_any, ids_any, green_any, send_ref, place_ref, green_ref, charge_ref, dest_ref, ids_ref, sems
):
    moves = [
        pltpu.make_async_copy(source, target, sems.at[n])
        for n, (source, target) in enumerate(
            [
                (dest_any, dest_ref),
                (ids_any, ids_ref),
                (charge_any, charge_ref),
                (green_any, green_ref),
            ]
        )
    ]
    for move in moves:
        move.start()
    moves[0].wait()
    dest = jnp.broadcast_to(dest_ref[...], (256, 256))
    row, col = iota((256, 256), 0), iota((256, 256), 1)
    dest_f = dest.astype(F32)
    dest_col = jnp.sum(jnp.where(row == col, dest_f, 0.0), axis=1, keepdims=True)
    earlier = (dest_col == dest_f) & (row < col)
    rank = jnp.sum(jnp.where(earlier, 1.0, 0.0), axis=0, keepdims=True)
    place_ref[...] = dest_f[0:1] * CAP + rank
    here = iota((128, 256), 0) == dest[:128]
    rank = jnp.broadcast_to(rank, (128, 256))
    moves[1].wait()
    ids = jnp.broadcast_to(ids_ref[...], (128, 256)).astype(F32)
    lane = iota((128, 128), 1)
    moves[3].wait()
    named = green_ref[:, 0, :]
    hots = []
    for slot in range(CAP):
        chosen = here & (rank == slot)
        hots.append(jnp.where(chosen, 1.0, 0.0).astype(BF))
        number = jnp.sum(jnp.where(chosen, ids + 1.0, 0.0), axis=1, keepdims=True) - 1.0
        named = jnp.where(lane == 9 + slot, number, named)
    moves[2].wait()
    parts = jnp.concatenate(three(charge_ref[...]), axis=1)
    moved = dot(jnp.concatenate(hots, axis=0), parts)
    moved = moved[:, :128] + moved[:, 128:256] + moved[:, 256:]
    for slot in range(CAP):
        send_ref[pl.ds(slot, 128, stride=5), :] = moved[slot * 128 : (slot + 1) * 128]
    send_ref[pl.ds(4, 128, stride=5), :] = named


def block_name(index):
    return (((index % 8) * 4 + (index // 8) % 4) * 8 + index // 32).astype(F32)


def slot_rows(r):
    first, count = (0, 8) if r == 0 else (8, 8) if r == 8 else (16 * r, 16)
    return [slice(b * 128 + first, b * 128 + first + count) for b in range(CYP)], count


def z_forward_kernel(recv_ref, mix_ref, wave_ref, out_ref, turned_ref):
    ends = recv_ref[pl.ds(4, 128, stride=5), :]
    names = ends.T
    block = block_name(iota((256, 128), 0))
    hots = [jnp.where(block == names[9 + s : 10 + s, :], 1.0, 0.0).astype(BF) for s in range(CAP)]
    rows = jnp.concatenate([recv_ref[pl.ds(s, 128, stride=5), :] for s in range(CAP)], axis=0)
    field = dot(jnp.concatenate(hots, axis=1), jnp.concatenate(three(rows), axis=1))
    field = field[:, :128] + field[:, 128:256] + field[:, 256:]
    high, low = two(field)
    mixed = dot(mix_ref[:1024], jnp.concatenate([high, low], axis=1))
    mixed = mixed[:, :128] + mixed[:, 128:] + dot(mix_ref[1024:], high)
    mixed = jnp.concatenate([mixed[:512], mixed[512:]], axis=1)
    for r in range(9):
        places, count = slot_rows(r)
        high, low = two(jnp.concatenate([mixed[place] for place in places], axis=0))
        block = dot(jnp.concatenate([high, low], axis=0), wave_ref[r * 256 : (r + 1) * 256, :])
        size = 4 * count
        block = block[:size, :128] + block[:size, 128:] + block[size:, :128]
        for b, place in enumerate(places):
            turned_ref[place, :] = block[b * count : (b + 1) * count]
    for b in range(CYP):
        out_ref[pl.ds(b, 128, stride=5), :] = turned_ref[b * 128 : (b + 1) * 128, :].T
    relayed = []
    for i in range(N_PX):
        source = 64 if i < 4 else 0
        rows = ends[source : source + 16]
        relayed.append(pltpu.roll(rows, 128 - 16 * i, 1) if i else rows)
    out_ref[pl.ds(4, 128, stride=5), :] = jnp.concatenate(relayed, axis=0)


def plane_kernel(spec_ref, *refs):
    pieces, refs = refs[:4], refs[4:]
    x_fwd_ref, x_back_ref, y_fwd_ref, y_back_ref, out_ref, green_ref, first_ref, second_ref, line_ref = refs
    me = lax.axis_index("px")
    half, place = me // 4, me % 4
    left, middle = iota((16, 128), 1) < 64, iota((16, 128), 1) == 64
    for n in range(4):
        start = pl.multiple_of(jnp.bitwise_xor(place, n) * 16, 16)
        last = pieces[n][64:80, :]
        for r in range(9):
            pair = pieces[n][r // 2 * 16 : (r // 2 + 1) * 16, :]
            swapped = pltpu.roll(pair, 64, 1)
            both = jnp.where(left, swapped, pair) if r % 2 else jnp.where(left, pair, swapped)
            both = jnp.where(middle, last[:, 64 + r : 65 + r], both)
            green_ref[r, pl.ds(start, 16), :] = both
    ends = spec_ref[pl.ds(4, 128, stride=5), :].T[:16]
    ends = jnp.where(left | middle, ends, pltpu.roll(ends, 64, 1))
    y_fwd, y_back, x_fwd, x_back = y_fwd_ref[half], y_back_ref[half], x_fwd_ref[...], x_back_ref[...]
    for i in range(N_PX):
        rows = jnp.concatenate([spec_ref[pl.ds(i * 80 + b, 16, stride=5), :] for b in range(CYP)], axis=0)
        line_ref[i * 128 : (i + 1) * 128, :] = turned_pair(rows)
    turned = halves(dot(line_ref[...], y_fwd), 128)
    for i in range(N_PX):
        for kk in range(16):
            row = i * 128 + kk * 8
            first_ref[kk, i * 8 : (i + 1) * 8, :] = turned[row : row + 8]
    top = iota((64, 128), 0) == 0
    for group in range(4):
        rows = jnp.concatenate([turned_pair(first_ref[group * 4 + n]) for n in range(4)], axis=0)
        full = halves(dot(rows, x_fwd), 128)
        scaled = []
        for n in range(4):
            r = RESIDUE[group * 4 + n]
            green = green_ref[r]
            other = jnp.where(top, ends[r : r + 1, :], green)
            scaled += [full[n * 128 : n * 128 + 64] * green, full[n * 128 + 64 : (n + 1) * 128] * other]
        high, low = two(jnp.concatenate(scaled, axis=0))
        cells = dot(jnp.concatenate([high, low], axis=1), x_back)
        for n in range(4):
            pair = cells[n * 128 : (n + 1) * 128].T
            second_ref[group * 4 + n] = pair[:64] + pair[64:]
    for i in range(N_PX):
        rows = jnp.concatenate([second_ref[kk, i * 8 : (i + 1) * 8, :] for kk in range(16)], axis=0)
        high, low = two(rows)
        pair = dot(y_back, jnp.concatenate([high, low], axis=1), 0, 1)
        out_ref[i * 64 : (i + 1) * 64, :] = pair[:64] + pair[64:]


def z_back_kernel(spec_ref, recv_ref, wave_hi_ref, wave_lo_ref, mix_hi_ref, mix_lo_ref, out_ref, turned_ref, line_ref):
    for b in range(CYP):
        turned_ref[b * 128 : (b + 1) * 128, :] = spec_ref[pl.ds(b, 128, stride=4), :].T
    for r in range(9):
        places, count = slot_rows(r)
        high, low = two(jnp.concatenate([turned_ref[place, :] for place in places], axis=0))
        rows = slice(r * 128, (r + 1) * 128)
        size = 4 * count
        block = dot(jnp.concatenate([high, low], axis=0), wave_hi_ref[rows, :])
        block = block[:size] + block[size:] + dot(high, wave_lo_ref[rows, :])
        for b, place in enumerate(places):
            part = block[b * count : (b + 1) * count]
            line_ref[place, :] = part[:, :128]
            line_ref[slice(place.start + 512, place.stop + 512), :] = part[:, 128:]
    high, low = two(line_ref[...])
    field = dot(mix_hi_ref[...], jnp.concatenate([high, low], axis=1))
    field = field[:, :128] + field[:, 128:] + dot(mix_lo_ref[...], high)
    block = block_name(iota((128, 256), 1))
    names = recv_ref[pl.ds(4, 128, stride=5), :]
    hots = [jnp.where(names[:, 9 + s : 10 + s] == block, 1.0, 0.0).astype(BF) for s in range(CAP)]
    rows = dot(jnp.concatenate(hots, axis=0), jnp.concatenate(three(field), axis=1))
    rows = rows[:, :128] + rows[:, 128:256] + rows[:, 256:]
    for s in range(CAP):
        out_ref[pl.ds(s, 128, stride=4), :] = rows[s * 128 : (s + 1) * 128]


def unpack_kernel(back_ref, place_ref, out_ref):
    row, col = iota((256, 256), 0), iota((256, 256), 1)
    place = jnp.broadcast_to(place_ref[...], (256, 256))
    place = jnp.sum(jnp.where(row == col, place, 0.0), axis=1, keepdims=True).astype(jnp.int32)
    hots = jnp.where(iota((256, 512), 1) == place, 1.0, 0.0).astype(BF)
    parts = jnp.concatenate(three(back_ref[...]), axis=1)
    rows = dot(hots, parts)
    out_ref[...] = rows[:, :128] + rows[:, 128:256] + rows[:, 256:]


def green_kernel(green_ref, *refs):
    out_refs, (turned_ref, piece_ref, sems) = refs[:4], refs[4:]
    me = lax.axis_index("px")
    starts = [
        pl.multiple_of((me - me % 4 + jnp.bitwise_xor(me % 4, n)) * 16, 16) for n in range(4)
    ]
    left = iota((16, 128), 1) < 64
    for k2 in range(16):
        turned_ref[...] = green_ref[:, k2, :].T
        for n in range(4):
            even = turned_ref[pl.ds(starts[n], 4, stride=2), :]
            odd = pltpu.roll(turned_ref[pl.ds(starts[n] + 1, 4, stride=2), :], 64, 1)
            piece_ref[n, pl.ds(k2, 4, stride=16), :] = jnp.where(left[:4], even, odd)
            piece_ref[n, pl.ds(k2 + 64, 1), :] = turned_ref[pl.ds(starts[n] + 8, 1), :]
    for n in range(4):
        ends = pltpu.roll(green_ref[64], 192 - starts[n], 1)
        piece_ref[n, 64:80, :] = jnp.where(left, piece_ref[n, 64:80, :], ends)
    stores = [pltpu.make_async_copy(piece_ref.at[n], out_refs[n], sems.at[n]) for n in range(4)]
    for move in stores:
        move.start()
    for move in stores:
        move.wait()


def table_kernel(*refs):
    tables, copies, sems = refs[:6], refs[6:12], refs[12]
    moves = [pltpu.make_async_copy(tables[n], copies[n], sems.at[n]) for n in range(6)]
    for move in moves:
        move.start()
    for move in moves:
        move.wait()


def call(kernel, shape, scratch=(), dtype=F32, **specs):
    return pl.pallas_call(
        kernel,
        **specs,
        out_shape=jax.tree.map(
            lambda s: jax.ShapeDtypeStruct(s, dtype) if isinstance(s, tuple) else s,
            shape,
            is_leaf=lambda s: isinstance(s, tuple),
        ),
        scratch_shapes=list(scratch),
        compiler_params=PARAMS,
        name=kernel.__name__,
    )


def all_to_all(x, axes):
    return lax.all_to_all(x, axes, split_axis=0, concat_axis=0, tiled=True)


def local(charge, dest, local_ids, green_hat):
    wave, mix = z_tables()
    mix_hi, mix_lo = split_table(mix)
    mix_both = np.concatenate([mix_hi.T, mix_lo.T], axis=0)
    wave_hi, wave_lo = split_table(wave.reshape(9 * 128, 256))
    wave_both = np.concatenate(split_table(wave.transpose(0, 2, 1).reshape(9 * 256, 128)), axis=1)
    x_fwd, x_back = stacked(pair_table(0))
    order = np.arange(64).reshape(N_PZ, CYP).T.reshape(64)
    y_fwd, y_back = (np.stack(tables) for tables in zip(stacked(pair_table(0)), stacked(pair_table(1))))
    y_fwd = y_fwd.reshape(2, 2, 64, 256)[:, :, order].reshape(2, 128, 256)

    charge, dest, local_ids, green_hat = (
        pltpu.with_memory_space_constraint(x, pltpu.HBM)
        for x in (charge, dest.reshape(1, 256), local_ids.reshape(1, 256), green_hat)
    )
    send, place, green_hat = call(
        pack_kernel,
        [(640, 128), (1, 256), (128, 16, 128)],
        [
            pltpu.VMEM((256, 128), F32),
            pltpu.VMEM((1, 256), jnp.int32),
            pltpu.VMEM((1, 256), jnp.int32),
            pltpu.SemaphoreType.DMA((4,)),
        ],
        in_specs=[HBM] * 4,
    )(charge, dest, local_ids, green_hat)
    recv = all_to_all(send.reshape(N_DEV, 1, 640), BOTH).reshape(640, 128)
    tables = [
        pltpu.with_memory_space_constraint(jnp.asarray(x), pltpu.HBM)
        for x in (mix_both, wave_both, x_fwd, x_back, y_fwd, y_back)
    ]
    pieces = call(
        green_kernel,
        [pltpu.HBM((80, 128), F32)] * 4,
        [pltpu.VMEM((128, 128), F32), pltpu.VMEM((4, 80, 128), F32), pltpu.SemaphoreType.DMA((4,))],
        out_specs=[HBM] * 4,
    )(green_hat)
    mix_both, wave_both, x_fwd, x_back, y_fwd, y_back = call(
        table_kernel,
        [jax.ShapeDtypeStruct(x.shape, BF) for x in tables],
        [pltpu.SemaphoreType.DMA((6,))],
        in_specs=[HBM] * 6,
    )(*tables)
    green = [pieces[0]]
    for n in range(1, 4):
        pairs = [(i, i // 4 * 4 + ((i % 4) ^ n)) for i in range(N_PX)]
        green.append(lax.ppermute(pieces[n], "px", pairs))
    recv, green = lax.optimization_barrier((recv, green))
    lines = call(z_forward_kernel, (640, 128), [pltpu.VMEM((512, 128), F32)])(recv, mix_both, wave_both)
    planes = all_to_all(lines.reshape(N_DEV, 1, 640), BOTH).reshape(640, 128)
    planes = call(
        plane_kernel,
        (512, 128),
        [
            pltpu.VMEM((9, 64, 128), F32),
            pltpu.VMEM((16, 64, 128), F32),
            pltpu.VMEM((16, 64, 128), F32),
            pltpu.VMEM((1024, 128), BF),
        ],
    )(planes, *green, x_fwd, x_back, y_fwd, y_back)
    lines = all_to_all(planes.reshape(N_DEV, 4, 128), BOTH).reshape(512, 128)
    rows = call(z_back_kernel, (512, 128), [pltpu.VMEM((512, 128), F32), pltpu.VMEM((1024, 128), F32)])(
        lines, recv, wave_hi, wave_lo, mix_hi, mix_lo
    )
    rows = all_to_all(rows.reshape(N_DEV, 4, 128), BOTH).reshape(512, 128)
    return call(unpack_kernel, (256, 128))(rows, place)


def solution(mesh):
    return jax.shard_map(
        local,
        mesh=mesh,
        in_specs=(
            P(BOTH, None),
            P(BOTH, None),
            P(BOTH),
            P(None, "px", "pz"),
        ),
        out_specs=P(BOTH, None),
        check_vma=False,
    )
```

```python
import jax
import jax.numpy as jnp
import ml_dtypes
import numpy as np
from jax import lax
from jax.experimental import pallas as pl
from jax.experimental.pallas import tpu as pltpu
from jax.sharding import PartitionSpec as P

CXP = 8
CYP = 4
CAP = 4
N_PX = 8
N_PZ = 16
N_DEV = 128
BOTH = ("px", "pz")
RESIDUE = [0, 8] + [g for g in range(1, 8) for _ in range(2)]
BF = jnp.bfloat16
F32 = jnp.float32
VMEM = pl.BlockSpec(memory_space=pltpu.VMEM)
HBM = pl.BlockSpec(memory_space=pltpu.HBM)
PARAMS = pltpu.CompilerParams(vmem_limit_bytes=16 << 20)


def split_table(table):
    high = table.astype(np.float32).astype(ml_dtypes.bfloat16)
    low = (table - high.astype(np.float64)).astype(ml_dtypes.bfloat16)
    return high, low


def z_tables():
    device = np.arange(N_DEV)
    q = 8 * (device % N_PZ) + device // N_PZ
    l = np.arange(128)
    wave = []
    for r in range(9):
        angle = 2.0 * np.pi * ((q[:, None] * 16 + r) * l[None, :] % 2048) / 2048.0
        wave.append(np.concatenate([np.cos(angle), np.sin(angle)], axis=1))
    wave = np.stack(wave)
    mix = np.zeros((8, 4, 8, 2, 4, 16, 8))
    for c in range(8):
        for kk in range(16):
            r = RESIDUE[kk]
            angle = 2.0 * np.pi * ((r * c) % 16) / 16.0
            if kk < 2:
                cosine_part, sine_part, weight = np.cos(angle), np.cos(angle), 1.0
            elif kk % 2 == 0:
                cosine_part, sine_part, weight = np.cos(angle), -np.sin(angle), 2.0
            else:
                cosine_part, sine_part, weight = np.sin(angle), np.cos(angle), 2.0
            scale = np.sqrt(weight / 2048.0)
            for b in range(4):
                for a in range(8):
                    mix[c, b, a, 0, b, kk, a] = cosine_part * scale
                    mix[c, b, a, 1, b, kk, a] = sine_part * scale
    return wave, mix.reshape(256, 1024)


def pair_table(half):
    k = 64 * half + np.arange(64)
    cell = np.arange(64)[:, None]
    cosine = np.cos(2.0 * np.pi * (cell * k[None, :] % 128) / 128.0) * np.sqrt(2.0)
    sine = np.sin(2.0 * np.pi * (cell * k[None, :] % 128) / 128.0) * np.sqrt(2.0)
    cosine[:, 0] = np.cos(np.pi * half * np.arange(64))
    sine[:, 0] = np.cos(np.pi * (1 - half) * np.arange(64))
    return np.concatenate([cosine, sine], axis=1) / np.sqrt(128.0)


def stacked(table):
    high, low = split_table(table)
    none = np.zeros_like(low)
    fwd = np.block([[high, low], [high, none]])
    back = np.block([[high.T, low.T], [high.T, none.T]])
    return fwd, back


def iota(shape, axis):
    return lax.broadcasted_iota(jnp.int32, shape, axis)


def two(x):
    high = x.astype(BF)
    return high, (x - high.astype(F32)).astype(BF)


def three(x):
    high = x.astype(BF)
    rest = x - high.astype(F32)
    middle = rest.astype(BF)
    return high, middle, (rest - middle.astype(F32)).astype(BF)


def turned_pair(x):
    high = x.astype(BF).astype(F32)
    return jnp.concatenate([high, x - high], axis=0).T.astype(BF)


def halves(x, size):
    return x[:, :size] + x[:, size:]


def dot(a, b, a_axis=1, b_axis=0):
    return lax.dot_general(a, b, (((a_axis,), (b_axis,)), ((), ())), preferred_element_type=F32)


def pack_kernel(
    charge_any, dest_any, ids_any, green_any, send_ref, place_ref, green_ref, charge_ref, dest_ref, ids_ref, sems
):
    moves = [
        pltpu.make_async_copy(source, target, sems.at[n])
        for n, (source, target) in enumerate(
            [
                (dest_any, dest_ref),
                (ids_any, ids_ref),
                (charge_any, charge_ref),
                (green_any.at[:72], green_ref),
            ]
        )
    ]
    for move in moves:
        move.start()
    moves[0].wait()
    dest = jnp.broadcast_to(dest_ref[...], (256, 256))
    row, col = iota((256, 256), 0), iota((256, 256), 1)
    dest_f = dest.astype(F32)
    dest_col = jnp.sum(jnp.where(row == col, dest_f, 0.0), axis=1, keepdims=True)
    earlier = (dest_col == dest_f) & (row < col)
    rank = jnp.sum(jnp.where(earlier, 1.0, 0.0), axis=0, keepdims=True)
    place_ref[...] = dest_f[0:1] * CAP + rank
    here = iota((128, 256), 0) == dest[:128]
    rank = jnp.broadcast_to(rank, (128, 256))
    moves[1].wait()
    ids = jnp.broadcast_to(ids_ref[...], (128, 256)).astype(F32)
    lane = iota((128, 128), 1)
    named = jnp.zeros((128, 128), F32)
    hots = []
    for slot in range(CAP):
        chosen = here & (rank == slot)
        hots.append(jnp.where(chosen, 1.0, 0.0).astype(BF))
        number = jnp.sum(jnp.where(chosen, ids + 1.0, 0.0), axis=1, keepdims=True) - 1.0
        named = jnp.where(lane == 9 + slot, number, named)
    moves[2].wait()
    parts = jnp.concatenate(three(charge_ref[...]), axis=1)
    moved = dot(jnp.concatenate(hots, axis=0), parts)
    moved = moved[:, :128] + moved[:, 128:256] + moved[:, 256:]
    for slot in range(CAP):
        send_ref[pl.ds(slot, 128, stride=5), :] = moved[slot * 128 : (slot + 1) * 128]
    moves[3].wait()
    plane = jnp.concatenate([green_ref[:, 0, :], jnp.zeros((56, 128), F32)], axis=0)
    send_ref[pl.ds(4, 128, stride=5), :] = jnp.where((lane >= 9) & (lane < 9 + CAP), named, plane)


def block_name(index):
    return (((index % 8) * 4 + (index // 8) % 4) * 8 + index // 32).astype(F32)


def slot_rows(r):
    first, count = (0, 8) if r == 0 else (8, 8) if r == 8 else (16 * r, 16)
    return [slice(b * 128 + first, b * 128 + first + count) for b in range(CYP)], count


def z_forward_kernel(recv_ref, mix_ref, wave_ref, out_ref, turned_ref):
    ends = recv_ref[pl.ds(4, 128, stride=5), :]
    names = ends.T
    block = block_name(iota((256, 128), 0))
    hots = [jnp.where(block == names[9 + s : 10 + s, :], 1.0, 0.0).astype(BF) for s in range(CAP)]
    rows = jnp.concatenate([recv_ref[pl.ds(s, 128, stride=5), :] for s in range(CAP)], axis=0)
    field = dot(jnp.concatenate(hots, axis=1), jnp.concatenate(three(rows), axis=1))
    field = field[:, :128] + field[:, 128:256] + field[:, 256:]
    high, low = two(field)
    mixed = dot(mix_ref[:1024], jnp.concatenate([high, low], axis=1))
    mixed = mixed[:, :128] + mixed[:, 128:] + dot(mix_ref[1024:], high)
    mixed = jnp.concatenate([mixed[:512], mixed[512:]], axis=1)
    for r in range(9):
        places, count = slot_rows(r)
        high, low = two(jnp.concatenate([mixed[place] for place in places], axis=0))
        block = dot(jnp.concatenate([high, low], axis=0), wave_ref[r * 256 : (r + 1) * 256, :])
        size = 4 * count
        block = block[:size, :128] + block[:size, 128:] + block[size:, :128]
        for b, place in enumerate(places):
            turned_ref[place, :] = block[b * count : (b + 1) * count]
    for b in range(CYP):
        out_ref[pl.ds(b, 128, stride=5), :] = turned_ref[b * 128 : (b + 1) * 128, :].T
    relayed = []
    for i in range(N_PX):
        source = 64 if i < 4 else 0
        rows = ends[source : source + 16]
        relayed.append(pltpu.roll(rows, 128 - 16 * i, 1) if i else rows)
    out_ref[pl.ds(4, 128, stride=5), :] = jnp.concatenate(relayed, axis=0)


def plane_kernel(spec_ref, *refs):
    pieces, refs = refs[:4], refs[4:]
    x_fwd_ref, x_back_ref, y_fwd_ref, y_back_ref, out_ref, green_ref, first_ref, second_ref, line_ref = refs
    me = lax.axis_index("px")
    half, place = me // 4, me % 4
    left, middle = iota((8, 128), 1) < 64, iota((8, 128), 1) == 64
    for n in range(4):
        start = pl.multiple_of(jnp.bitwise_xor(place, n) * 16, 16)
        last = pieces[n][72:80, :]
        for r in range(9):
            pair = pieces[n][r * 8 : (r + 1) * 8, :]
            swapped = pltpu.roll(pair, 64, 1)
            low = jnp.where(middle, last[:, r : r + 1], jnp.where(left, pair, swapped))
            high = jnp.where(middle, last[:, 64 + r : 65 + r], jnp.where(left, swapped, pair))
            green_ref[r, pl.ds(start, 16), :] = jnp.concatenate([low, high], axis=0)
    ends = spec_ref[pl.ds(4, 128, stride=5), :].T[:16]
    lane = iota((16, 128), 1)
    ends = jnp.where(lane <= 64, ends, pltpu.roll(ends, 64, 1))
    y_fwd, y_back, x_fwd, x_back = y_fwd_ref[half], y_back_ref[half], x_fwd_ref[...], x_back_ref[...]
    for i in range(N_PX):
        rows = jnp.concatenate([spec_ref[pl.ds(i * 80 + b, 16, stride=5), :] for b in range(CYP)], axis=0)
        line_ref[i * 128 : (i + 1) * 128, :] = turned_pair(rows)
    turned = halves(dot(line_ref[...], y_fwd), 128)
    for i in range(N_PX):
        for kk in range(16):
            row = i * 128 + kk * 8
            first_ref[kk, i * 8 : (i + 1) * 8, :] = turned[row : row + 8]
    top = iota((64, 128), 0) == 0
    for group in range(4):
        rows = jnp.concatenate([turned_pair(first_ref[group * 4 + n]) for n in range(4)], axis=0)
        full = halves(dot(rows, x_fwd), 128)
        scaled = []
        for n in range(4):
            r = RESIDUE[group * 4 + n]
            green = green_ref[r]
            other = jnp.where(top, ends[r : r + 1, :], green)
            scaled += [full[n * 128 : n * 128 + 64] * green, full[n * 128 + 64 : (n + 1) * 128] * other]
        high, low = two(jnp.concatenate(scaled, axis=0))
        cells = dot(jnp.concatenate([high, low], axis=1), x_back)
        for n in range(4):
            pair = cells[n * 128 : (n + 1) * 128].T
            second_ref[group * 4 + n] = pair[:64] + pair[64:]
    for i in range(N_PX):
        rows = jnp.concatenate([second_ref[kk, i * 8 : (i + 1) * 8, :] for kk in range(16)], axis=0)
        high, low = two(rows)
        pair = dot(y_back, jnp.concatenate([high, low], axis=1), 0, 1)
        out_ref[i * 64 : (i + 1) * 64, :] = pair[:64] + pair[64:]


def z_back_kernel(spec_ref, recv_ref, wave_hi_ref, wave_lo_ref, mix_hi_ref, mix_lo_ref, out_ref, turned_ref, line_ref):
    for b in range(CYP):
        turned_ref[b * 128 : (b + 1) * 128, :] = spec_ref[pl.ds(b, 128, stride=4), :].T
    for r in range(9):
        places, count = slot_rows(r)
        high, low = two(jnp.concatenate([turned_ref[place, :] for place in places], axis=0))
        rows = slice(r * 128, (r + 1) * 128)
        size = 4 * count
        block = dot(jnp.concatenate([high, low], axis=0), wave_hi_ref[rows, :])
        block = block[:size] + block[size:] + dot(high, wave_lo_ref[rows, :])
        for b, place in enumerate(places):
            part = block[b * count : (b + 1) * count]
            line_ref[place, :] = part[:, :128]
            line_ref[slice(place.start + 512, place.stop + 512), :] = part[:, 128:]
    high, low = two(line_ref[...])
    field = dot(mix_hi_ref[...], jnp.concatenate([high, low], axis=1))
    field = field[:, :128] + field[:, 128:] + dot(mix_lo_ref[...], high)
    block = block_name(iota((128, 256), 1))
    names = recv_ref[pl.ds(4, 128, stride=5), :]
    hots = [jnp.where(names[:, 9 + s : 10 + s] == block, 1.0, 0.0).astype(BF) for s in range(CAP)]
    rows = dot(jnp.concatenate(hots, axis=0), jnp.concatenate(three(field), axis=1))
    rows = rows[:, :128] + rows[:, 128:256] + rows[:, 256:]
    for s in range(CAP):
        out_ref[pl.ds(s, 128, stride=4), :] = rows[s * 128 : (s + 1) * 128]


def unpack_kernel(back_ref, place_ref, out_ref):
    row, col = iota((256, 256), 0), iota((256, 256), 1)
    place = jnp.broadcast_to(place_ref[...], (256, 256))
    place = jnp.sum(jnp.where(row == col, place, 0.0), axis=1, keepdims=True).astype(jnp.int32)
    hots = jnp.where(iota((256, 512), 1) == place, 1.0, 0.0).astype(BF)
    parts = jnp.concatenate(three(back_ref[...]), axis=1)
    rows = dot(hots, parts)
    out_ref[...] = rows[:, :128] + rows[:, 128:256] + rows[:, 256:]


def green_kernel(green_ref, *refs):
    out_refs, (turned_ref, piece_ref, sems) = refs[:4], refs[4:]
    me = lax.axis_index("px")
    starts = [
        pl.multiple_of((me - me % 4 + jnp.bitwise_xor(me % 4, n)) * 16, 16) for n in range(4)
    ]
    left = iota((8, 128), 1) < 64
    for k2 in range(8):
        both = jnp.concatenate([green_ref[:64, k2, :], green_ref[:64, k2 + 8, :]], axis=0)
        turned_ref[...] = both.T
        for n in range(4):
            piece_ref[n, pl.ds(k2, 8, stride=8), :] = turned_ref[pl.ds(starts[n], 8), :]
            piece_ref[n, 64 + k2 : 65 + k2, :] = turned_ref[pl.ds(starts[n] + 8, 1), :]
    middle = green_ref[64]
    for n in range(4):
        low = pltpu.roll(middle[:8], 128 - starts[n], 1)
        high = pltpu.roll(middle[8:], 192 - starts[n], 1)
        piece_ref[n, 72:80, :] = jnp.where(left, low, high)
    stores = [pltpu.make_async_copy(piece_ref.at[n], out_refs[n], sems.at[n]) for n in range(4)]
    for move in stores:
        move.start()
    for move in stores:
        move.wait()


def table_kernel(*refs):
    tables, copies, sems = refs[:6], refs[6:12], refs[12]
    moves = [pltpu.make_async_copy(tables[n], copies[n], sems.at[n]) for n in range(6)]
    for move in moves:
        move.start()
    for move in moves:
        move.wait()


def call(kernel, shape, scratch=(), dtype=F32, **specs):
    return pl.pallas_call(
        kernel,
        **specs,
        out_shape=jax.tree.map(
            lambda s: jax.ShapeDtypeStruct(s, dtype) if isinstance(s, tuple) else s,
            shape,
            is_leaf=lambda s: isinstance(s, tuple),
        ),
        scratch_shapes=list(scratch),
        compiler_params=PARAMS,
        name=kernel.__name__,
    )


def all_to_all(x, axes):
    return lax.all_to_all(x, axes, split_axis=0, concat_axis=0, tiled=True)


def local(charge, dest, local_ids, green_hat):
    wave, mix = z_tables()
    mix_hi, mix_lo = split_table(mix)
    mix_both = np.concatenate([mix_hi.T, mix_lo.T], axis=0)
    wave_hi, wave_lo = split_table(wave.reshape(9 * 128, 256))
    wave_both = np.concatenate(split_table(wave.transpose(0, 2, 1).reshape(9 * 256, 128)), axis=1)
    x_fwd, x_back = stacked(pair_table(0))
    order = np.arange(64).reshape(N_PZ, CYP).T.reshape(64)
    y_fwd, y_back = (np.stack(tables) for tables in zip(stacked(pair_table(0)), stacked(pair_table(1))))
    y_fwd = y_fwd.reshape(2, 2, 64, 256)[:, :, order].reshape(2, 128, 256)

    charge, dest, local_ids, green_hat = (
        pltpu.with_memory_space_constraint(x, pltpu.HBM)
        for x in (charge, dest.reshape(1, 256), local_ids.reshape(1, 256), green_hat)
    )
    send, place, green_hat = call(
        pack_kernel,
        [(640, 128), (1, 256), (72, 16, 128)],
        [
            pltpu.VMEM((256, 128), F32),
            pltpu.VMEM((1, 256), jnp.int32),
            pltpu.VMEM((1, 256), jnp.int32),
            pltpu.SemaphoreType.DMA((4,)),
        ],
        in_specs=[HBM] * 4,
    )(charge, dest, local_ids, green_hat)
    recv = all_to_all(send.reshape(N_DEV, 1, 640), BOTH).reshape(640, 128)
    tables = [
        pltpu.with_memory_space_constraint(jnp.asarray(x), pltpu.HBM)
        for x in (mix_both, wave_both, x_fwd, x_back, y_fwd, y_back)
    ]
    pieces = call(
        green_kernel,
        [pltpu.HBM((80, 128), F32)] * 4,
        [pltpu.VMEM((128, 128), F32), pltpu.VMEM((4, 80, 128), F32), pltpu.SemaphoreType.DMA((4,))],
        out_specs=[HBM] * 4,
    )(green_hat)
    mix_both, wave_both, x_fwd, x_back, y_fwd, y_back = call(
        table_kernel,
        [jax.ShapeDtypeStruct(x.shape, BF) for x in tables],
        [pltpu.SemaphoreType.DMA((6,))],
        in_specs=[HBM] * 6,
    )(*tables)
    green = [pieces[0]]
    for n in range(1, 4):
        pairs = [(i, i // 4 * 4 + ((i % 4) ^ n)) for i in range(N_PX)]
        green.append(lax.ppermute(pieces[n], "px", pairs))
    recv, green = lax.optimization_barrier((recv, green))
    lines = call(z_forward_kernel, (640, 128), [pltpu.VMEM((512, 128), F32)])(recv, mix_both, wave_both)
    planes = all_to_all(lines.reshape(N_DEV, 1, 640), BOTH).reshape(640, 128)
    planes = call(
        plane_kernel,
        (512, 128),
        [
            pltpu.VMEM((9, 64, 128), F32),
            pltpu.VMEM((16, 64, 128), F32),
            pltpu.VMEM((16, 64, 128), F32),
            pltpu.VMEM((1024, 128), BF),
        ],
    )(planes, *green, x_fwd, x_back, y_fwd, y_back)
    lines = all_to_all(planes.reshape(N_DEV, 4, 128), BOTH).reshape(512, 128)
    rows = call(z_back_kernel, (512, 128), [pltpu.VMEM((512, 128), F32), pltpu.VMEM((1024, 128), F32)])(
        lines, recv, wave_hi, wave_lo, mix_hi, mix_lo
    )
    rows = all_to_all(rows.reshape(N_DEV, 4, 128), BOTH).reshape(512, 128)
    return call(unpack_kernel, (256, 128))(rows, place)


def solution(mesh):
    return jax.shard_map(
        local,
        mesh=mesh,
        in_specs=(
            P(BOTH, None),
            P(BOTH, None),
            P(BOTH),
            P(None, "px", "pz"),
        ),
        out_specs=P(BOTH, None),
        check_vma=False,
    )
```

```python
import jax
import jax.numpy as jnp
import ml_dtypes
import numpy as np
from jax import lax
from jax.experimental import pallas as pl
from jax.experimental.pallas import tpu as pltpu
from jax.sharding import PartitionSpec as P

CXP = 8
CYP = 4
CAP = 4
N_PX = 8
N_PZ = 16
N_DEV = 128
BOTH = ("px", "pz")
RESIDUE = [0, 8] + [g for g in range(1, 8) for _ in range(2)]
BF = jnp.bfloat16
F32 = jnp.float32
VMEM = pl.BlockSpec(memory_space=pltpu.VMEM)
HBM = pl.BlockSpec(memory_space=pltpu.HBM)
PARAMS = pltpu.CompilerParams(vmem_limit_bytes=16 << 20)


def split_table(table):
    high = table.astype(np.float32).astype(ml_dtypes.bfloat16)
    low = (table - high.astype(np.float64)).astype(ml_dtypes.bfloat16)
    return high, low


def z_tables():
    device = np.arange(N_DEV)
    q = 8 * (device % N_PZ) + device // N_PZ
    l = np.arange(128)
    wave = []
    for r in range(9):
        angle = 2.0 * np.pi * ((q[:, None] * 16 + r) * l[None, :] % 2048) / 2048.0
        wave.append(np.concatenate([np.cos(angle), np.sin(angle)], axis=1))
    wave = np.stack(wave)
    mix = np.zeros((8, 4, 8, 2, 4, 16, 8))
    for c in range(8):
        for kk in range(16):
            r = RESIDUE[kk]
            angle = 2.0 * np.pi * ((r * c) % 16) / 16.0
            if kk < 2:
                cosine_part, sine_part, weight = np.cos(angle), np.cos(angle), 1.0
            elif kk % 2 == 0:
                cosine_part, sine_part, weight = np.cos(angle), -np.sin(angle), 2.0
            else:
                cosine_part, sine_part, weight = np.sin(angle), np.cos(angle), 2.0
            scale = np.sqrt(weight / 2048.0)
            for b in range(4):
                for a in range(8):
                    mix[c, b, a, 0, b, kk, a] = cosine_part * scale
                    mix[c, b, a, 1, b, kk, a] = sine_part * scale
    return wave, mix.reshape(256, 1024)


def pair_table(half):
    k = 64 * half + np.arange(64)
    cell = np.arange(64)[:, None]
    cosine = np.cos(2.0 * np.pi * (cell * k[None, :] % 128) / 128.0) * np.sqrt(2.0)
    sine = np.sin(2.0 * np.pi * (cell * k[None, :] % 128) / 128.0) * np.sqrt(2.0)
    cosine[:, 0] = np.cos(np.pi * half * np.arange(64))
    sine[:, 0] = np.cos(np.pi * (1 - half) * np.arange(64))
    return np.concatenate([cosine, sine], axis=1) / np.sqrt(128.0)


def stacked(table):
    high, low = split_table(table)
    none = np.zeros_like(low)
    fwd = np.block([[high, low], [high, none]])
    back = np.block([[high.T, low.T], [high.T, none.T]])
    return fwd, back


def iota(shape, axis):
    return lax.broadcasted_iota(jnp.int32, shape, axis)


def two(x):
    high = x.astype(BF)
    return high, (x - high.astype(F32)).astype(BF)


def three(x):
    high = x.astype(BF)
    rest = x - high.astype(F32)
    middle = rest.astype(BF)
    return high, middle, (rest - middle.astype(F32)).astype(BF)


def turned_pair(x):
    high = x.astype(BF).astype(F32)
    return jnp.concatenate([high, x - high], axis=0).T.astype(BF)


def halves(x, size):
    return x[:, :size] + x[:, size:]


def dot(a, b, a_axis=1, b_axis=0):
    return lax.dot_general(a, b, (((a_axis,), (b_axis,)), ((), ())), preferred_element_type=F32)


def pack_kernel(
    charge_any, dest_any, ids_any, green_any, send_ref, place_ref, green_ref, charge_ref, dest_ref, ids_ref, sems
):
    moves = [
        pltpu.make_async_copy(source, target, sems.at[n])
        for n, (source, target) in enumerate(
            [
                (dest_any, dest_ref),
                (ids_any, ids_ref),
                (charge_any, charge_ref),
                (green_any.at[:72], green_ref),
            ]
        )
    ]
    for move in moves:
        move.start()
    moves[0].wait()
    dest = jnp.broadcast_to(dest_ref[...], (256, 256))
    row, col = iota((256, 256), 0), iota((256, 256), 1)
    dest_f = dest.astype(F32)
    dest_col = jnp.sum(jnp.where(row == col, dest_f, 0.0), axis=1, keepdims=True)
    earlier = (dest_col == dest_f) & (row < col)
    rank = jnp.sum(jnp.where(earlier, 1.0, 0.0), axis=0, keepdims=True)
    place_ref[...] = dest_f[0:1] * CAP + rank
    here = iota((128, 256), 0) == dest[:128]
    rank = jnp.broadcast_to(rank, (128, 256))
    moves[1].wait()
    ids = jnp.broadcast_to(ids_ref[...], (128, 256)).astype(F32)
    lane = iota((128, 128), 1)
    named = jnp.zeros((128, 128), F32)
    hots = []
    for slot in range(CAP):
        chosen = here & (rank == slot)
        hots.append(jnp.where(chosen, 1.0, 0.0).astype(BF))
        number = jnp.sum(jnp.where(chosen, ids + 1.0, 0.0), axis=1, keepdims=True) - 1.0
        named = jnp.where(lane == 9 + slot, number, named)
    moves[2].wait()
    parts = jnp.concatenate(three(charge_ref[...]), axis=1)
    moved = dot(jnp.concatenate(hots, axis=0), parts)
    moved = moved[:, :128] + moved[:, 128:256] + moved[:, 256:]
    for slot in range(CAP):
        send_ref[pl.ds(slot, 128, stride=5), :] = moved[slot * 128 : (slot + 1) * 128]
    moves[3].wait()
    plane = jnp.concatenate([green_ref[:, 0, :], jnp.zeros((56, 128), F32)], axis=0)
    send_ref[pl.ds(4, 128, stride=5), :] = jnp.where((lane >= 9) & (lane < 9 + CAP), named, plane)


def block_name(index):
    return (((index % 8) * 4 + (index // 8) % 4) * 8 + index // 32).astype(F32)


def slot_rows(r):
    first, count = (0, 8) if r == 0 else (8, 8) if r == 8 else (16 * r, 16)
    return [slice(b * 128 + first, b * 128 + first + count) for b in range(CYP)], count


def scatter_kernel(recv_ref, mix_ref, mixed_ref):
    ends = recv_ref[pl.ds(4, 128, stride=5), :]
    names = ends.T
    block = block_name(iota((256, 128), 0))
    hots = [jnp.where(block == names[9 + s : 10 + s, :], 1.0, 0.0).astype(BF) for s in range(CAP)]
    rows = jnp.concatenate([recv_ref[pl.ds(s, 128, stride=5), :] for s in range(CAP)], axis=0)
    field = dot(jnp.concatenate(hots, axis=1), jnp.concatenate(three(rows), axis=1))
    field = field[:, :128] + field[:, 128:256] + field[:, 256:]
    high, low = two(field)
    mixed = dot(mix_ref[:1024], jnp.concatenate([high, low], axis=1))
    mixed = mixed[:, :128] + mixed[:, 128:] + dot(mix_ref[1024:], high)
    mixed_ref[:, :128] = mixed[:512]
    mixed_ref[:, 128:] = mixed[512:]


def z_forward_kernel(mixed_ref, recv_ref, wave_ref, out_ref, turned_ref):
    ends = recv_ref[pl.ds(4, 128, stride=5), :]
    mixed = mixed_ref[...]
    for r in range(9):
        places, count = slot_rows(r)
        high, low = two(jnp.concatenate([mixed[place] for place in places], axis=0))
        block = dot(jnp.concatenate([high, low], axis=0), wave_ref[r * 256 : (r + 1) * 256, :])
        size = 4 * count
        block = block[:size, :128] + block[:size, 128:] + block[size:, :128]
        for b, place in enumerate(places):
            turned_ref[place, :] = block[b * count : (b + 1) * count]
    for b in range(CYP):
        out_ref[pl.ds(b, 128, stride=5), :] = turned_ref[b * 128 : (b + 1) * 128, :].T
    relayed = []
    for i in range(N_PX):
        source = 64 if i < 4 else 0
        rows = ends[source : source + 16]
        relayed.append(pltpu.roll(rows, 128 - 16 * i, 1) if i else rows)
    out_ref[pl.ds(4, 128, stride=5), :] = jnp.concatenate(relayed, axis=0)


def plane_kernel(spec_ref, *refs):
    pieces, refs = refs[:4], refs[4:]
    x_fwd_ref, x_back_ref, y_fwd_ref, y_back_ref, out_ref, green_ref, first_ref, second_ref, line_ref = refs
    me = lax.axis_index("px")
    half, place = me // 4, me % 4
    left, middle = iota((8, 128), 1) < 64, iota((8, 128), 1) == 64
    for n in range(4):
        start = pl.multiple_of(jnp.bitwise_xor(place, n) * 16, 16)
        last = pieces[n][72:80, :]
        for r in range(9):
            pair = pieces[n][r * 8 : (r + 1) * 8, :]
            swapped = pltpu.roll(pair, 64, 1)
            low = jnp.where(middle, last[:, r : r + 1], jnp.where(left, pair, swapped))
            high = jnp.where(middle, last[:, 64 + r : 65 + r], jnp.where(left, swapped, pair))
            green_ref[r, pl.ds(start, 16), :] = jnp.concatenate([low, high], axis=0)
    ends = spec_ref[pl.ds(4, 128, stride=5), :].T[:16]
    lane = iota((16, 128), 1)
    ends = jnp.where(lane <= 64, ends, pltpu.roll(ends, 64, 1))
    y_fwd, y_back, x_fwd, x_back = y_fwd_ref[half], y_back_ref[half], x_fwd_ref[...], x_back_ref[...]
    for i in range(N_PX):
        rows = jnp.concatenate([spec_ref[pl.ds(i * 80 + b, 16, stride=5), :] for b in range(CYP)], axis=0)
        line_ref[i * 128 : (i + 1) * 128, :] = turned_pair(rows)
    turned = halves(dot(line_ref[...], y_fwd), 128)
    for i in range(N_PX):
        for kk in range(16):
            row = i * 128 + kk * 8
            first_ref[kk, i * 8 : (i + 1) * 8, :] = turned[row : row + 8]
    top = iota((64, 128), 0) == 0
    for group in range(4):
        rows = jnp.concatenate([turned_pair(first_ref[group * 4 + n]) for n in range(4)], axis=0)
        full = halves(dot(rows, x_fwd), 128)
        scaled = []
        for n in range(4):
            r = RESIDUE[group * 4 + n]
            green = green_ref[r]
            other = jnp.where(top, ends[r : r + 1, :], green)
            scaled += [full[n * 128 : n * 128 + 64] * green, full[n * 128 + 64 : (n + 1) * 128] * other]
        high, low = two(jnp.concatenate(scaled, axis=0))
        cells = dot(jnp.concatenate([high, low], axis=1), x_back)
        for n in range(4):
            pair = cells[n * 128 : (n + 1) * 128].T
            second_ref[group * 4 + n] = pair[:64] + pair[64:]
    for i in range(N_PX):
        rows = jnp.concatenate([second_ref[kk, i * 8 : (i + 1) * 8, :] for kk in range(16)], axis=0)
        high, low = two(rows)
        pair = dot(y_back, jnp.concatenate([high, low], axis=1), 0, 1)
        out_ref[i * 64 : (i + 1) * 64, :] = pair[:64] + pair[64:]


def z_back_kernel(spec_ref, recv_ref, wave_hi_ref, wave_lo_ref, mix_hi_ref, mix_lo_ref, out_ref, turned_ref, line_ref):
    for b in range(CYP):
        turned_ref[b * 128 : (b + 1) * 128, :] = spec_ref[pl.ds(b, 128, stride=4), :].T
    for r in range(9):
        places, count = slot_rows(r)
        high, low = two(jnp.concatenate([turned_ref[place, :] for place in places], axis=0))
        rows = slice(r * 128, (r + 1) * 128)
        size = 4 * count
        block = dot(jnp.concatenate([high, low], axis=0), wave_hi_ref[rows, :])
        block = block[:size] + block[size:] + dot(high, wave_lo_ref[rows, :])
        for b, place in enumerate(places):
            part = block[b * count : (b + 1) * count]
            line_ref[place, :] = part[:, :128]
            line_ref[slice(place.start + 512, place.stop + 512), :] = part[:, 128:]
    high, low = two(line_ref[...])
    field = dot(mix_hi_ref[...], jnp.concatenate([high, low], axis=1))
    field = field[:, :128] + field[:, 128:] + dot(mix_lo_ref[...], high)
    block = block_name(iota((128, 256), 1))
    names = recv_ref[pl.ds(4, 128, stride=5), :]
    hots = [jnp.where(names[:, 9 + s : 10 + s] == block, 1.0, 0.0).astype(BF) for s in range(CAP)]
    rows = dot(jnp.concatenate(hots, axis=0), jnp.concatenate(three(field), axis=1))
    rows = rows[:, :128] + rows[:, 128:256] + rows[:, 256:]
    for s in range(CAP):
        out_ref[pl.ds(s, 128, stride=4), :] = rows[s * 128 : (s + 1) * 128]


def unpack_kernel(back_ref, place_ref, out_ref):
    row, col = iota((256, 256), 0), iota((256, 256), 1)
    place = jnp.broadcast_to(place_ref[...], (256, 256))
    place = jnp.sum(jnp.where(row == col, place, 0.0), axis=1, keepdims=True).astype(jnp.int32)
    hots = jnp.where(iota((256, 512), 1) == place, 1.0, 0.0).astype(BF)
    parts = jnp.concatenate(three(back_ref[...]), axis=1)
    rows = dot(hots, parts)
    out_ref[...] = rows[:, :128] + rows[:, 128:256] + rows[:, 256:]


def green_kernel(green_ref, *refs):
    out_refs, (turned_ref, piece_ref, sems) = refs[:4], refs[4:]
    me = lax.axis_index("px")
    starts = [
        pl.multiple_of((me - me % 4 + jnp.bitwise_xor(me % 4, n)) * 16, 16) for n in range(4)
    ]
    left = iota((8, 128), 1) < 64
    for k2 in range(8):
        both = jnp.concatenate([green_ref[:64, k2, :], green_ref[:64, k2 + 8, :]], axis=0)
        turned_ref[...] = both.T
        for n in range(4):
            piece_ref[n, pl.ds(k2, 8, stride=8), :] = turned_ref[pl.ds(starts[n], 8), :]
            piece_ref[n, 64 + k2 : 65 + k2, :] = turned_ref[pl.ds(starts[n] + 8, 1), :]
    middle = green_ref[64]
    for n in range(4):
        low = pltpu.roll(middle[:8], 128 - starts[n], 1)
        high = pltpu.roll(middle[8:], 192 - starts[n], 1)
        piece_ref[n, 72:80, :] = jnp.where(left, low, high)
    stores = [pltpu.make_async_copy(piece_ref.at[n], out_refs[n], sems.at[n]) for n in range(4)]
    for move in stores:
        move.start()
    for move in stores:
        move.wait()


def table_kernel(*refs):
    tables, copies, sems = refs[:6], refs[6:12], refs[12]
    moves = [pltpu.make_async_copy(tables[n], copies[n], sems.at[n]) for n in range(6)]
    for move in moves:
        move.start()
    for move in moves:
        move.wait()


def call(kernel, shape, scratch=(), dtype=F32, **specs):
    return pl.pallas_call(
        kernel,
        **specs,
        out_shape=jax.tree.map(
            lambda s: jax.ShapeDtypeStruct(s, dtype) if isinstance(s, tuple) else s,
            shape,
            is_leaf=lambda s: isinstance(s, tuple),
        ),
        scratch_shapes=list(scratch),
        compiler_params=PARAMS,
        name=kernel.__name__,
    )


def all_to_all(x, axes):
    return lax.all_to_all(x, axes, split_axis=0, concat_axis=0, tiled=True)


def local(charge, dest, local_ids, green_hat):
    wave, mix = z_tables()
    mix_hi, mix_lo = split_table(mix)
    mix_both = np.concatenate([mix_hi.T, mix_lo.T], axis=0)
    wave_hi, wave_lo = split_table(wave.reshape(9 * 128, 256))
    wave_both = np.concatenate(split_table(wave.transpose(0, 2, 1).reshape(9 * 256, 128)), axis=1)
    x_fwd, x_back = stacked(pair_table(0))
    order = np.arange(64).reshape(N_PZ, CYP).T.reshape(64)
    y_fwd, y_back = (np.stack(tables) for tables in zip(stacked(pair_table(0)), stacked(pair_table(1))))
    y_fwd = y_fwd.reshape(2, 2, 64, 256)[:, :, order].reshape(2, 128, 256)

    charge, dest, local_ids, green_hat = (
        pltpu.with_memory_space_constraint(x, pltpu.HBM)
        for x in (charge, dest.reshape(1, 256), local_ids.reshape(1, 256), green_hat)
    )
    send, place, green_hat = call(
        pack_kernel,
        [(640, 128), (1, 256), (72, 16, 128)],
        [
            pltpu.VMEM((256, 128), F32),
            pltpu.VMEM((1, 256), jnp.int32),
            pltpu.VMEM((1, 256), jnp.int32),
            pltpu.SemaphoreType.DMA((4,)),
        ],
        in_specs=[HBM] * 4,
    )(charge, dest, local_ids, green_hat)
    recv = all_to_all(send.reshape(N_DEV, 1, 640), BOTH).reshape(640, 128)
    tables = [
        pltpu.with_memory_space_constraint(jnp.asarray(x), pltpu.HBM)
        for x in (mix_both, wave_both, x_fwd, x_back, y_fwd, y_back)
    ]
    pieces = call(
        green_kernel,
        [pltpu.HBM((80, 128), F32)] * 4,
        [pltpu.VMEM((128, 128), F32), pltpu.VMEM((4, 80, 128), F32), pltpu.SemaphoreType.DMA((4,))],
        out_specs=[HBM] * 4,
    )(green_hat)
    mix_both, wave_both, x_fwd, x_back, y_fwd, y_back = call(
        table_kernel,
        [jax.ShapeDtypeStruct(x.shape, BF) for x in tables],
        [pltpu.SemaphoreType.DMA((6,))],
        in_specs=[HBM] * 6,
    )(*tables)
    green = [pieces[0]]
    for n in range(1, 4):
        pairs = [(i, i // 4 * 4 + ((i % 4) ^ n)) for i in range(N_PX)]
        green.append(lax.ppermute(pieces[n], "px", pairs))
    mixed = call(scatter_kernel, (512, 256))(recv, mix_both)
    mixed, green = lax.optimization_barrier((mixed, green))
    lines = call(z_forward_kernel, (640, 128), [pltpu.VMEM((512, 128), F32)])(mixed, recv, wave_both)
    planes = all_to_all(lines.reshape(N_DEV, 1, 640), BOTH).reshape(640, 128)
    planes = call(
        plane_kernel,
        (512, 128),
        [
            pltpu.VMEM((9, 64, 128), F32),
            pltpu.VMEM((16, 64, 128), F32),
            pltpu.VMEM((16, 64, 128), F32),
            pltpu.VMEM((1024, 128), BF),
        ],
    )(planes, *green, x_fwd, x_back, y_fwd, y_back)
    lines = all_to_all(planes.reshape(N_DEV, 4, 128), BOTH).reshape(512, 128)
    rows = call(z_back_kernel, (512, 128), [pltpu.VMEM((512, 128), F32), pltpu.VMEM((1024, 128), F32)])(
        lines, recv, wave_hi, wave_lo, mix_hi, mix_lo
    )
    rows = all_to_all(rows.reshape(N_DEV, 4, 128), BOTH).reshape(512, 128)
    return call(unpack_kernel, (256, 128))(rows, place)


def solution(mesh):
    return jax.shard_map(
        local,
        mesh=mesh,
        in_specs=(
            P(BOTH, None),
            P(BOTH, None),
            P(BOTH),
            P(None, "px", "pz"),
        ),
        out_specs=P(BOTH, None),
        check_vma=False,
    )
```

```python
import jax
import jax.numpy as jnp
import ml_dtypes
import numpy as np
from jax import lax
from jax.experimental import pallas as pl
from jax.experimental.pallas import tpu as pltpu
from jax.sharding import PartitionSpec as P

CXP = 8
CYP = 4
CAP = 4
N_PX = 8
N_PZ = 16
N_DEV = 128
BOTH = ("px", "pz")
RESIDUE = [0, 8] + [g for g in range(1, 8) for _ in range(2)]
BF = jnp.bfloat16
F32 = jnp.float32
VMEM = pl.BlockSpec(memory_space=pltpu.VMEM)
HBM = pl.BlockSpec(memory_space=pltpu.HBM)
PARAMS = pltpu.CompilerParams(vmem_limit_bytes=16 << 20)


def split_table(table):
    high = table.astype(np.float32).astype(ml_dtypes.bfloat16)
    low = (table - high.astype(np.float64)).astype(ml_dtypes.bfloat16)
    return high, low


def z_tables():
    device = np.arange(N_DEV)
    q = 8 * (device % N_PZ) + device // N_PZ
    l = np.arange(128)
    wave = []
    for r in range(9):
        angle = 2.0 * np.pi * ((q[:, None] * 16 + r) * l[None, :] % 2048) / 2048.0
        wave.append(np.concatenate([np.cos(angle), np.sin(angle)], axis=1))
    wave = np.stack(wave)
    mix = np.zeros((8, 4, 8, 2, 4, 16, 8))
    for c in range(8):
        for kk in range(16):
            r = RESIDUE[kk]
            angle = 2.0 * np.pi * ((r * c) % 16) / 16.0
            if kk < 2:
                cosine_part, sine_part, weight = np.cos(angle), np.cos(angle), 1.0
            elif kk % 2 == 0:
                cosine_part, sine_part, weight = np.cos(angle), -np.sin(angle), 2.0
            else:
                cosine_part, sine_part, weight = np.sin(angle), np.cos(angle), 2.0
            scale = np.sqrt(weight / 2048.0)
            for b in range(4):
                for a in range(8):
                    mix[c, b, a, 0, b, kk, a] = cosine_part * scale
                    mix[c, b, a, 1, b, kk, a] = sine_part * scale
    return wave, mix.reshape(256, 1024)


def pair_table(half):
    k = 64 * half + np.arange(64)
    cell = np.arange(64)[:, None]
    cosine = np.cos(2.0 * np.pi * (cell * k[None, :] % 128) / 128.0) * np.sqrt(2.0)
    sine = np.sin(2.0 * np.pi * (cell * k[None, :] % 128) / 128.0) * np.sqrt(2.0)
    cosine[:, 0] = np.cos(np.pi * half * np.arange(64))
    sine[:, 0] = np.cos(np.pi * (1 - half) * np.arange(64))
    return np.concatenate([cosine, sine], axis=1) / np.sqrt(128.0)


def stacked(table):
    high, low = split_table(table)
    none = np.zeros_like(low)
    fwd = np.block([[high, low], [high, none]])
    back = np.block([[high.T, low.T], [high.T, none.T]])
    return fwd, back


def iota(shape, axis):
    return lax.broadcasted_iota(jnp.int32, shape, axis)


def two(x):
    high = x.astype(BF)
    return high, (x - high.astype(F32)).astype(BF)


def three(x):
    high = x.astype(BF)
    rest = x - high.astype(F32)
    middle = rest.astype(BF)
    return high, middle, (rest - middle.astype(F32)).astype(BF)


def turned_pair(x):
    high = x.astype(BF).astype(F32)
    return jnp.concatenate([high, x - high], axis=0).T.astype(BF)


def halves(x, size):
    return x[:, :size] + x[:, size:]


def dot(a, b, a_axis=1, b_axis=0):
    return lax.dot_general(a, b, (((a_axis,), (b_axis,)), ((), ())), preferred_element_type=F32)


def pack_kernel(
    charge_any, dest_any, ids_any, green_any, send_ref, place_ref, green_ref, charge_ref, dest_ref, ids_ref, sems
):
    moves = [
        pltpu.make_async_copy(source, target, sems.at[n])
        for n, (source, target) in enumerate(
            [
                (dest_any, dest_ref),
                (ids_any, ids_ref),
                (charge_any, charge_ref),
                (green_any.at[:72], green_ref),
            ]
        )
    ]
    for move in moves:
        move.start()
    moves[0].wait()
    dest = jnp.broadcast_to(dest_ref[...], (256, 256))
    row, col = iota((256, 256), 0), iota((256, 256), 1)
    dest_f = dest.astype(F32)
    dest_col = jnp.sum(jnp.where(row == col, dest_f, 0.0), axis=1, keepdims=True)
    earlier = (dest_col == dest_f) & (row < col)
    rank = jnp.sum(jnp.where(earlier, 1.0, 0.0), axis=0, keepdims=True)
    place_ref[...] = dest_f[0:1] * CAP + rank
    here = iota((128, 256), 0) == dest[:128]
    rank = jnp.broadcast_to(rank, (128, 256))
    moves[1].wait()
    ids = jnp.broadcast_to(ids_ref[...], (128, 256)).astype(F32)
    lane = iota((128, 128), 1)
    named = jnp.zeros((128, 128), F32)
    hots = []
    for slot in range(CAP):
        chosen = here & (rank == slot)
        hots.append(jnp.where(chosen, 1.0, 0.0).astype(BF))
        number = jnp.sum(jnp.where(chosen, ids + 1.0, 0.0), axis=1, keepdims=True) - 1.0
        named = jnp.where(lane == 9 + slot, number, named)
    moves[2].wait()
    parts = jnp.concatenate(three(charge_ref[...]), axis=1)
    moved = dot(jnp.concatenate(hots, axis=0), parts)
    moved = moved[:, :128] + moved[:, 128:256] + moved[:, 256:]
    for slot in range(CAP):
        send_ref[pl.ds(slot, 128, stride=5), :] = moved[slot * 128 : (slot + 1) * 128]
    moves[3].wait()
    plane = jnp.concatenate([green_ref[:, 0, :], jnp.zeros((56, 128), F32)], axis=0)
    send_ref[pl.ds(4, 128, stride=5), :] = jnp.where((lane >= 9) & (lane < 9 + CAP), named, plane)


def block_name(index):
    return (((index % 8) * 4 + (index // 8) % 4) * 8 + index // 32).astype(F32)


def slot_rows(r):
    first, count = (0, 8) if r == 0 else (8, 8) if r == 8 else (16 * r, 16)
    return [slice(b * 128 + first, b * 128 + first + count) for b in range(CYP)], count


def z_forward_kernel(recv_ref, mix_ref, wave_ref, out_ref, turned_ref):
    ends = recv_ref[pl.ds(4, 128, stride=5), :]
    names = ends.T
    block = block_name(iota((256, 128), 0))
    hots = [jnp.where(block == names[9 + s : 10 + s, :], 1.0, 0.0).astype(BF) for s in range(CAP)]
    rows = jnp.concatenate([recv_ref[pl.ds(s, 128, stride=5), :] for s in range(CAP)], axis=0)
    field = dot(jnp.concatenate(hots, axis=1), jnp.concatenate(three(rows), axis=1))
    field = field[:, :128] + field[:, 128:256] + field[:, 256:]
    high, low = two(field)
    mixed = dot(mix_ref[:1024], jnp.concatenate([high, low], axis=1))
    mixed = mixed[:, :128] + mixed[:, 128:] + dot(mix_ref[1024:], high)
    mixed = jnp.concatenate([mixed[:512], mixed[512:]], axis=1)
    for r in range(9):
        places, count = slot_rows(r)
        high, low = two(jnp.concatenate([mixed[place] for place in places], axis=0))
        block = dot(jnp.concatenate([high, low], axis=0), wave_ref[r * 256 : (r + 1) * 256, :])
        size = 4 * count
        block = block[:size, :128] + block[:size, 128:] + block[size:, :128]
        for b, place in enumerate(places):
            turned_ref[place, :] = block[b * count : (b + 1) * count]
    for b in range(CYP):
        out_ref[pl.ds(b, 128, stride=5), :] = turned_ref[b * 128 : (b + 1) * 128, :].T
    relayed = []
    for i in range(N_PX):
        source = 64 if i < 4 else 0
        rows = ends[source : source + 16]
        relayed.append(pltpu.roll(rows, 128 - 16 * i, 1) if i else rows)
    out_ref[pl.ds(4, 128, stride=5), :] = jnp.concatenate(relayed, axis=0)


def plane_kernel(spec_ref, *refs):
    pieces, refs = refs[:4], refs[4:]
    x_fwd_ref, x_back_ref, y_fwd_ref, y_back_ref, out_ref, green_ref, first_ref, second_ref, line_ref = refs
    me = lax.axis_index("px")
    half, place = me // 4, me % 4
    left, middle = iota((8, 128), 1) < 64, iota((8, 128), 1) == 64
    for n in range(4):
        start = pl.multiple_of(jnp.bitwise_xor(place, n) * 16, 16)
        last = pieces[n][72:80, :]
        for r in range(9):
            pair = pieces[n][r * 8 : (r + 1) * 8, :]
            swapped = pltpu.roll(pair, 64, 1)
            low = jnp.where(middle, last[:, r : r + 1], jnp.where(left, pair, swapped))
            high = jnp.where(middle, last[:, 64 + r : 65 + r], jnp.where(left, swapped, pair))
            green_ref[r, pl.ds(start, 16), :] = jnp.concatenate([low, high], axis=0)
    ends = spec_ref[pl.ds(4, 128, stride=5), :].T[:16]
    lane = iota((16, 128), 1)
    ends = jnp.where(lane <= 64, ends, pltpu.roll(ends, 64, 1))
    y_fwd, y_back, x_fwd, x_back = y_fwd_ref[half], y_back_ref[half], x_fwd_ref[...], x_back_ref[...]
    for i in range(N_PX):
        rows = jnp.concatenate([spec_ref[pl.ds(i * 80 + b, 16, stride=5), :] for b in range(CYP)], axis=0)
        line_ref[i * 128 : (i + 1) * 128, :] = turned_pair(rows)
    turned = halves(dot(line_ref[...], y_fwd), 128)
    for i in range(N_PX):
        for kk in range(16):
            row = i * 128 + kk * 8
            first_ref[kk, i * 8 : (i + 1) * 8, :] = turned[row : row + 8]
    top = iota((64, 128), 0) == 0
    for group in range(4):
        rows = jnp.concatenate([turned_pair(first_ref[group * 4 + n]) for n in range(4)], axis=0)
        full = halves(dot(rows, x_fwd), 128)
        scaled = []
        for n in range(4):
            r = RESIDUE[group * 4 + n]
            green = green_ref[r]
            other = jnp.where(top, ends[r : r + 1, :], green)
            scaled += [full[n * 128 : n * 128 + 64] * green, full[n * 128 + 64 : (n + 1) * 128] * other]
        high, low = two(jnp.concatenate(scaled, axis=0))
        cells = dot(jnp.concatenate([high, low], axis=1), x_back)
        for n in range(4):
            pair = cells[n * 128 : (n + 1) * 128].T
            second_ref[group * 4 + n] = pair[:64] + pair[64:]
    for i in range(N_PX):
        rows = jnp.concatenate([second_ref[kk, i * 8 : (i + 1) * 8, :] for kk in range(16)], axis=0)
        high, low = two(rows)
        pair = dot(y_back, jnp.concatenate([high, low], axis=1), 0, 1)
        out_ref[i * 64 : (i + 1) * 64, :] = pair[:64] + pair[64:]


def z_back_kernel(spec_ref, recv_ref, wave_hi_ref, wave_lo_ref, mix_hi_ref, mix_lo_ref, out_ref, turned_ref, line_ref):
    for b in range(CYP):
        turned_ref[b * 128 : (b + 1) * 128, :] = spec_ref[pl.ds(b, 128, stride=4), :].T
    for r in range(9):
        places, count = slot_rows(r)
        high, low = two(jnp.concatenate([turned_ref[place, :] for place in places], axis=0))
        rows = slice(r * 128, (r + 1) * 128)
        size = 4 * count
        block = dot(jnp.concatenate([high, low], axis=0), wave_hi_ref[rows, :])
        block = block[:size] + block[size:] + dot(high, wave_lo_ref[rows, :])
        for b, place in enumerate(places):
            part = block[b * count : (b + 1) * count]
            line_ref[place, :] = part[:, :128]
            line_ref[slice(place.start + 512, place.stop + 512), :] = part[:, 128:]
    high, low = two(line_ref[...])
    field = dot(mix_hi_ref[...], jnp.concatenate([high, low], axis=1))
    field = field[:, :128] + field[:, 128:] + dot(mix_lo_ref[...], high)
    block = block_name(iota((128, 256), 1))
    names = recv_ref[pl.ds(4, 128, stride=5), :]
    hots = [jnp.where(names[:, 9 + s : 10 + s] == block, 1.0, 0.0).astype(BF) for s in range(CAP)]
    rows = dot(jnp.concatenate(hots, axis=0), jnp.concatenate(three(field), axis=1))
    rows = rows[:, :128] + rows[:, 128:256] + rows[:, 256:]
    for s in range(CAP):
        out_ref[pl.ds(s, 128, stride=4), :] = rows[s * 128 : (s + 1) * 128]


def unpack_kernel(back_ref, place_ref, out_ref):
    row, col = iota((256, 256), 0), iota((256, 256), 1)
    place = jnp.broadcast_to(place_ref[...], (256, 256))
    place = jnp.sum(jnp.where(row == col, place, 0.0), axis=1, keepdims=True).astype(jnp.int32)
    hots = jnp.where(iota((256, 512), 1) == place, 1.0, 0.0).astype(BF)
    parts = jnp.concatenate(three(back_ref[...]), axis=1)
    rows = dot(hots, parts)
    out_ref[...] = rows[:, :128] + rows[:, 128:256] + rows[:, 256:]


def green_kernel(green_ref, *refs):
    out_refs, (turned_ref, piece_ref, sems) = refs[:4], refs[4:]
    me = lax.axis_index("px")
    starts = [
        pl.multiple_of((me - me % 4 + jnp.bitwise_xor(me % 4, n)) * 16, 16) for n in range(4)
    ]
    left = iota((8, 128), 1) < 64
    for k2 in range(8):
        both = jnp.concatenate([green_ref[:64, k2, :], green_ref[:64, k2 + 8, :]], axis=0)
        turned_ref[...] = both.T
        for n in range(4):
            piece_ref[n, pl.ds(k2, 8, stride=8), :] = turned_ref[pl.ds(starts[n], 8), :]
            piece_ref[n, 64 + k2 : 65 + k2, :] = turned_ref[pl.ds(starts[n] + 8, 1), :]
    middle = green_ref[64]
    for n in range(4):
        low = pltpu.roll(middle[:8], 128 - starts[n], 1)
        high = pltpu.roll(middle[8:], 192 - starts[n], 1)
        piece_ref[n, 72:80, :] = jnp.where(left, low, high)
    stores = [pltpu.make_async_copy(piece_ref.at[n], out_refs[n], sems.at[n]) for n in range(4)]
    for move in stores:
        move.start()
    for move in stores:
        move.wait()


def table_kernel(*refs):
    tables, copies, sems = refs[:6], refs[6:12], refs[12]
    moves = [pltpu.make_async_copy(tables[n], copies[n], sems.at[n]) for n in range(6)]
    for move in moves:
        move.start()
    for move in moves:
        move.wait()


def call(kernel, shape, scratch=(), dtype=F32, **specs):
    return pl.pallas_call(
        kernel,
        **specs,
        out_shape=jax.tree.map(
            lambda s: jax.ShapeDtypeStruct(s, dtype) if isinstance(s, tuple) else s,
            shape,
            is_leaf=lambda s: isinstance(s, tuple),
        ),
        scratch_shapes=list(scratch),
        compiler_params=PARAMS,
        name=kernel.__name__,
    )


def all_to_all(x, axes):
    return lax.all_to_all(x, axes, split_axis=0, concat_axis=0, tiled=True)


def local(charge, dest, local_ids, green_hat):
    wave, mix = z_tables()
    mix_hi, mix_lo = split_table(mix)
    mix_both = np.concatenate([mix_hi.T, mix_lo.T], axis=0)
    wave_hi, wave_lo = split_table(wave.reshape(9 * 128, 256))
    wave_both = np.concatenate(split_table(wave.transpose(0, 2, 1).reshape(9 * 256, 128)), axis=1)
    x_fwd, x_back = stacked(pair_table(0))
    order = np.arange(64).reshape(N_PZ, CYP).T.reshape(64)
    y_fwd, y_back = (np.stack(tables) for tables in zip(stacked(pair_table(0)), stacked(pair_table(1))))
    y_fwd = y_fwd.reshape(2, 2, 64, 256)[:, :, order].reshape(2, 128, 256)

    charge, dest, local_ids, green_hat = (
        pltpu.with_memory_space_constraint(x, pltpu.HBM)
        for x in (charge, dest.reshape(1, 256), local_ids.reshape(1, 256), green_hat)
    )
    send, place, green_hat = call(
        pack_kernel,
        [(640, 128), (1, 256), (72, 16, 128)],
        [
            pltpu.VMEM((256, 128), F32),
            pltpu.VMEM((1, 256), jnp.int32),
            pltpu.VMEM((1, 256), jnp.int32),
            pltpu.SemaphoreType.DMA((4,)),
        ],
        in_specs=[HBM] * 4,
    )(charge, dest, local_ids, green_hat)
    recv = all_to_all(send.reshape(N_DEV, 1, 640), BOTH).reshape(640, 128)
    tables = [
        pltpu.with_memory_space_constraint(jnp.asarray(x), pltpu.HBM)
        for x in (mix_both, wave_both, x_fwd, x_back, y_fwd, y_back)
    ]
    pieces = call(
        green_kernel,
        [pltpu.HBM((80, 128), F32)] * 4,
        [pltpu.VMEM((128, 128), F32), pltpu.VMEM((4, 80, 128), F32), pltpu.SemaphoreType.DMA((4,))],
        out_specs=[HBM] * 4,
    )(green_hat)
    mix_both, wave_both, x_fwd, x_back, y_fwd, y_back = call(
        table_kernel,
        [jax.ShapeDtypeStruct(x.shape, BF) for x in tables],
        [pltpu.SemaphoreType.DMA((6,))],
        in_specs=[HBM] * 6,
    )(*tables)
    green = [pieces[0]]
    for n in range(1, 4):
        pairs = [(i, i // 4 * 4 + ((i % 4) ^ n)) for i in range(N_PX)]
        green.append(lax.ppermute(pieces[n], "px", pairs))
    lines = call(z_forward_kernel, (640, 128), [pltpu.VMEM((512, 128), F32)])(recv, mix_both, wave_both)
    lines, green = lax.optimization_barrier((lines, green))
    planes = all_to_all(lines.reshape(N_DEV, 1, 640), BOTH).reshape(640, 128)
    planes = call(
        plane_kernel,
        (512, 128),
        [
            pltpu.VMEM((9, 64, 128), F32),
            pltpu.VMEM((16, 64, 128), F32),
            pltpu.VMEM((16, 64, 128), F32),
            pltpu.VMEM((1024, 128), BF),
        ],
    )(planes, *green, x_fwd, x_back, y_fwd, y_back)
    lines = all_to_all(planes.reshape(N_DEV, 4, 128), BOTH).reshape(512, 128)
    rows = call(z_back_kernel, (512, 128), [pltpu.VMEM((512, 128), F32), pltpu.VMEM((1024, 128), F32)])(
        lines, recv, wave_hi, wave_lo, mix_hi, mix_lo
    )
    rows = all_to_all(rows.reshape(N_DEV, 4, 128), BOTH).reshape(512, 128)
    return call(unpack_kernel, (256, 128))(rows, place)


def solution(mesh):
    return jax.shard_map(
        local,
        mesh=mesh,
        in_specs=(
            P(BOTH, None),
            P(BOTH, None),
            P(BOTH),
            P(None, "px", "pz"),
        ),
        out_specs=P(BOTH, None),
        check_vma=False,
    )
```

```python
import jax
import jax.numpy as jnp
import ml_dtypes
import numpy as np
from jax import lax
from jax.experimental import pallas as pl
from jax.experimental.pallas import tpu as pltpu
from jax.sharding import PartitionSpec as P

CXP = 8
CYP = 4
CAP = 4
N_PX = 8
N_PZ = 16
N_DEV = 128
BOTH = ("px", "pz")
RESIDUE = [0, 8] + [g for g in range(1, 8) for _ in range(2)]
BF = jnp.bfloat16
F32 = jnp.float32
VMEM = pl.BlockSpec(memory_space=pltpu.VMEM)
HBM = pl.BlockSpec(memory_space=pltpu.HBM)
PARAMS = pltpu.CompilerParams(vmem_limit_bytes=16 << 20)


def split_table(table):
    high = table.astype(np.float32).astype(ml_dtypes.bfloat16)
    low = (table - high.astype(np.float64)).astype(ml_dtypes.bfloat16)
    return high, low


def z_tables():
    device = np.arange(N_DEV)
    q = 8 * (device % N_PZ) + device // N_PZ
    l = np.arange(128)
    wave = []
    for r in range(9):
        angle = 2.0 * np.pi * ((q[:, None] * 16 + r) * l[None, :] % 2048) / 2048.0
        wave.append(np.concatenate([np.cos(angle), np.sin(angle)], axis=1))
    wave = np.stack(wave)
    mix = np.zeros((8, 4, 8, 2, 4, 16, 8))
    for c in range(8):
        for kk in range(16):
            r = RESIDUE[kk]
            angle = 2.0 * np.pi * ((r * c) % 16) / 16.0
            if kk < 2:
                cosine_part, sine_part, weight = np.cos(angle), np.cos(angle), 1.0
            elif kk % 2 == 0:
                cosine_part, sine_part, weight = np.cos(angle), -np.sin(angle), 2.0
            else:
                cosine_part, sine_part, weight = np.sin(angle), np.cos(angle), 2.0
            scale = np.sqrt(weight / 2048.0)
            for b in range(4):
                for a in range(8):
                    mix[c, b, a, 0, b, kk, a] = cosine_part * scale
                    mix[c, b, a, 1, b, kk, a] = sine_part * scale
    return wave, mix.reshape(256, 1024)


def pair_table(half):
    k = 64 * half + np.arange(64)
    cell = np.arange(64)[:, None]
    cosine = np.cos(2.0 * np.pi * (cell * k[None, :] % 128) / 128.0) * np.sqrt(2.0)
    sine = np.sin(2.0 * np.pi * (cell * k[None, :] % 128) / 128.0) * np.sqrt(2.0)
    cosine[:, 0] = np.cos(np.pi * half * np.arange(64))
    sine[:, 0] = np.cos(np.pi * (1 - half) * np.arange(64))
    return np.concatenate([cosine, sine], axis=1) / np.sqrt(128.0)


def stacked(table):
    high, low = split_table(table)
    none = np.zeros_like(low)
    fwd = np.block([[high, low], [high, none]])
    back = np.block([[high.T, low.T], [high.T, none.T]])
    return fwd, back


def iota(shape, axis):
    return lax.broadcasted_iota(jnp.int32, shape, axis)


def two(x):
    high = x.astype(BF)
    return high, (x - high.astype(F32)).astype(BF)


def three(x):
    high = x.astype(BF)
    rest = x - high.astype(F32)
    middle = rest.astype(BF)
    return high, middle, (rest - middle.astype(F32)).astype(BF)


def turned_pair(x):
    high = x.astype(BF).astype(F32)
    return jnp.concatenate([high, x - high], axis=0).T.astype(BF)


def halves(x, size):
    return x[:, :size] + x[:, size:]


def dot(a, b, a_axis=1, b_axis=0):
    return lax.dot_general(a, b, (((a_axis,), (b_axis,)), ((), ())), preferred_element_type=F32)


def pack_kernel(
    charge_any, dest_any, ids_any, green_any, send_ref, place_ref, green_ref, charge_ref, dest_ref, ids_ref, sems
):
    moves = [
        pltpu.make_async_copy(source, target, sems.at[n])
        for n, (source, target) in enumerate(
            [
                (dest_any, dest_ref),
                (ids_any, ids_ref),
                (charge_any, charge_ref),
                (green_any.at[:72], green_ref),
            ]
        )
    ]
    for move in moves:
        move.start()
    moves[0].wait()
    dest = jnp.broadcast_to(dest_ref[...], (256, 256))
    row, col = iota((256, 256), 0), iota((256, 256), 1)
    dest_f = dest.astype(F32)
    dest_col = jnp.sum(jnp.where(row == col, dest_f, 0.0), axis=1, keepdims=True)
    earlier = (dest_col == dest_f) & (row < col)
    rank = jnp.sum(jnp.where(earlier, 1.0, 0.0), axis=0, keepdims=True)
    place_ref[...] = dest_f[0:1] * CAP + rank
    here = iota((128, 256), 0) == dest[:128]
    rank = jnp.broadcast_to(rank, (128, 256))
    moves[1].wait()
    ids = jnp.broadcast_to(ids_ref[...], (128, 256)).astype(F32)
    lane = iota((128, 128), 1)
    named = jnp.zeros((128, 128), F32)
    hots = []
    for slot in range(CAP):
        chosen = here & (rank == slot)
        hots.append(jnp.where(chosen, 1.0, 0.0).astype(BF))
        number = jnp.sum(jnp.where(chosen, ids + 1.0, 0.0), axis=1, keepdims=True) - 1.0
        named = jnp.where(lane == 9 + slot, number, named)
    moves[2].wait()
    parts = jnp.concatenate(three(charge_ref[...]), axis=1)
    moved = dot(jnp.concatenate(hots, axis=0), parts)
    moved = moved[:, :128] + moved[:, 128:256] + moved[:, 256:]
    for slot in range(CAP):
        send_ref[pl.ds(slot, 128, stride=5), :] = moved[slot * 128 : (slot + 1) * 128]
    moves[3].wait()
    plane = jnp.concatenate([green_ref[:, 0, :], jnp.zeros((56, 128), F32)], axis=0)
    send_ref[pl.ds(4, 128, stride=5), :] = jnp.where((lane >= 9) & (lane < 9 + CAP), named, plane)


def block_name(index):
    return (((index % 8) * 4 + (index // 8) % 4) * 8 + index // 32).astype(F32)


def slot_rows(r):
    first, count = (0, 8) if r == 0 else (8, 8) if r == 8 else (16 * r, 16)
    return [slice(b * 128 + first, b * 128 + first + count) for b in range(CYP)], count


def z_forward_kernel(recv_ref, mix_ref, wave_ref, out_ref, turned_ref):
    ends = recv_ref[pl.ds(4, 128, stride=5), :]
    names = ends.T
    block = block_name(iota((256, 128), 0))
    hots = [jnp.where(block == names[9 + s : 10 + s, :], 1.0, 0.0).astype(BF) for s in range(CAP)]
    rows = jnp.concatenate([recv_ref[pl.ds(s, 128, stride=5), :] for s in range(CAP)], axis=0)
    field = dot(jnp.concatenate(hots, axis=1), jnp.concatenate(three(rows), axis=1))
    field = field[:, :128] + field[:, 128:256] + field[:, 256:]
    high, low = two(field)
    mixed = dot(mix_ref[:1024], jnp.concatenate([high, low], axis=1))
    mixed = mixed[:, :128] + mixed[:, 128:] + dot(mix_ref[1024:], high)
    mixed = jnp.concatenate([mixed[:512], mixed[512:]], axis=1)
    for r in range(9):
        places, count = slot_rows(r)
        high, low = two(jnp.concatenate([mixed[place] for place in places], axis=0))
        block = dot(jnp.concatenate([high, low], axis=0), wave_ref[r * 256 : (r + 1) * 256, :])
        size = 4 * count
        block = block[:size, :128] + block[:size, 128:] + block[size:, :128]
        for b, place in enumerate(places):
            turned_ref[place, :] = block[b * count : (b + 1) * count]
    for b in range(CYP):
        out_ref[pl.ds(b, 128, stride=5), :] = turned_ref[b * 128 : (b + 1) * 128, :].T
    relayed = []
    for i in range(N_PX):
        source = 64 if i < 4 else 0
        rows = ends[source : source + 16]
        relayed.append(pltpu.roll(rows, 128 - 16 * i, 1) if i else rows)
    out_ref[pl.ds(4, 128, stride=5), :] = jnp.concatenate(relayed, axis=0)


def plane_kernel(spec_ref, *refs):
    pieces, refs = refs[:4], refs[4:]
    x_fwd_ref, x_back_ref, y_fwd_ref, y_back_ref, out_ref, green_ref, first_ref, second_ref = refs
    me = lax.axis_index("px")
    half, place = me // 4, me % 4
    left, middle = iota((8, 128), 1) < 64, iota((8, 128), 1) == 64
    for n in range(4):
        start = pl.multiple_of(jnp.bitwise_xor(place, n) * 16, 16)
        last = pieces[n][72:80, :]
        for r in range(9):
            pair = pieces[n][r * 8 : (r + 1) * 8, :]
            swapped = pltpu.roll(pair, 64, 1)
            low = jnp.where(middle, last[:, r : r + 1], jnp.where(left, pair, swapped))
            high = jnp.where(middle, last[:, 64 + r : 65 + r], jnp.where(left, swapped, pair))
            green_ref[r, pl.ds(start, 16), :] = jnp.concatenate([low, high], axis=0)
    ends = spec_ref[pl.ds(4, 128, stride=5), :].T[:16]
    lane = iota((16, 128), 1)
    ends = jnp.where(lane <= 64, ends, pltpu.roll(ends, 64, 1))
    y_fwd, y_back, x_fwd, x_back = y_fwd_ref[half], y_back_ref[half], x_fwd_ref[...], x_back_ref[...]
    for pair in range(4):
        rows = []
        for i in (2 * pair, 2 * pair + 1):
            cells = [spec_ref[pl.ds(i * 80 + b, 16, stride=5), :] for b in range(CYP)]
            rows.append(turned_pair(jnp.concatenate(cells, axis=0)))
        turned = halves(dot(jnp.concatenate(rows, axis=0), y_fwd), 128)
        for kk in range(16):
            first_ref[kk, pair * 16 : pair * 16 + 8, :] = turned[kk * 8 : kk * 8 + 8]
            first_ref[kk, pair * 16 + 8 : pair * 16 + 16, :] = turned[128 + kk * 8 : 136 + kk * 8]
    top = iota((64, 128), 0) == 0
    for group in range(4):
        rows = jnp.concatenate([turned_pair(first_ref[group * 4 + n]) for n in range(4)], axis=0)
        full = halves(dot(rows, x_fwd), 128)
        scaled = []
        for n in range(4):
            r = RESIDUE[group * 4 + n]
            green = green_ref[r]
            other = jnp.where(top, ends[r : r + 1, :], green)
            scaled += [full[n * 128 : n * 128 + 64] * green, full[n * 128 + 64 : (n + 1) * 128] * other]
        high, low = two(jnp.concatenate(scaled, axis=0))
        cells = dot(jnp.concatenate([high, low], axis=1), x_back)
        for n in range(4):
            pair = cells[n * 128 : (n + 1) * 128].T
            second_ref[group * 4 + n] = pair[:64] + pair[64:]
    for i in range(N_PX):
        rows = jnp.concatenate([second_ref[kk, i * 8 : (i + 1) * 8, :] for kk in range(16)], axis=0)
        high, low = two(rows)
        pair = dot(y_back, jnp.concatenate([high, low], axis=1), 0, 1)
        out_ref[i * 64 : (i + 1) * 64, :] = pair[:64] + pair[64:]


def z_back_kernel(spec_ref, recv_ref, wave_hi_ref, wave_lo_ref, mix_hi_ref, mix_lo_ref, out_ref, turned_ref, line_ref):
    for b in range(CYP):
        turned_ref[b * 128 : (b + 1) * 128, :] = spec_ref[pl.ds(b, 128, stride=4), :].T
    for r in range(9):
        places, count = slot_rows(r)
        high, low = two(jnp.concatenate([turned_ref[place, :] for place in places], axis=0))
        rows = slice(r * 128, (r + 1) * 128)
        size = 4 * count
        block = dot(jnp.concatenate([high, low], axis=0), wave_hi_ref[rows, :])
        block = block[:size] + block[size:] + dot(high, wave_lo_ref[rows, :])
        for b, place in enumerate(places):
            part = block[b * count : (b + 1) * count]
            line_ref[place, :] = part[:, :128]
            line_ref[slice(place.start + 512, place.stop + 512), :] = part[:, 128:]
    high, low = two(line_ref[...])
    field = dot(mix_hi_ref[...], jnp.concatenate([high, low], axis=1))
    field = field[:, :128] + field[:, 128:] + dot(mix_lo_ref[...], high)
    block = block_name(iota((128, 256), 1))
    names = recv_ref[pl.ds(4, 128, stride=5), :]
    hots = [jnp.where(names[:, 9 + s : 10 + s] == block, 1.0, 0.0).astype(BF) for s in range(CAP)]
    rows = dot(jnp.concatenate(hots, axis=0), jnp.concatenate(three(field), axis=1))
    rows = rows[:, :128] + rows[:, 128:256] + rows[:, 256:]
    for s in range(CAP):
        out_ref[pl.ds(s, 128, stride=4), :] = rows[s * 128 : (s + 1) * 128]


def unpack_kernel(back_ref, place_ref, out_ref):
    row, col = iota((256, 256), 0), iota((256, 256), 1)
    place = jnp.broadcast_to(place_ref[...], (256, 256))
    place = jnp.sum(jnp.where(row == col, place, 0.0), axis=1, keepdims=True).astype(jnp.int32)
    hots = jnp.where(iota((256, 512), 1) == place, 1.0, 0.0).astype(BF)
    parts = jnp.concatenate(three(back_ref[...]), axis=1)
    rows = dot(hots, parts)
    out_ref[...] = rows[:, :128] + rows[:, 128:256] + rows[:, 256:]


def green_kernel(green_ref, *refs):
    out_refs, (turned_ref, piece_ref, sems) = refs[:4], refs[4:]
    me = lax.axis_index("px")
    starts = [
        pl.multiple_of((me - me % 4 + jnp.bitwise_xor(me % 4, n)) * 16, 16) for n in range(4)
    ]
    left = iota((8, 128), 1) < 64
    for k2 in range(8):
        both = jnp.concatenate([green_ref[:64, k2, :], green_ref[:64, k2 + 8, :]], axis=0)
        turned_ref[...] = both.T
        for n in range(4):
            piece_ref[n, pl.ds(k2, 8, stride=8), :] = turned_ref[pl.ds(starts[n], 8), :]
            piece_ref[n, 64 + k2 : 65 + k2, :] = turned_ref[pl.ds(starts[n] + 8, 1), :]
    middle = green_ref[64]
    for n in range(4):
        low = pltpu.roll(middle[:8], 128 - starts[n], 1)
        high = pltpu.roll(middle[8:], 192 - starts[n], 1)
        piece_ref[n, 72:80, :] = jnp.where(left, low, high)
    stores = [pltpu.make_async_copy(piece_ref.at[n], out_refs[n], sems.at[n]) for n in range(4)]
    for move in stores:
        move.start()
    for move in stores:
        move.wait()


def table_kernel(*refs):
    tables, copies, sems = refs[:6], refs[6:12], refs[12]
    moves = [pltpu.make_async_copy(tables[n], copies[n], sems.at[n]) for n in range(6)]
    for move in moves:
        move.start()
    for move in moves:
        move.wait()


def call(kernel, shape, scratch=(), dtype=F32, **specs):
    return pl.pallas_call(
        kernel,
        **specs,
        out_shape=jax.tree.map(
            lambda s: jax.ShapeDtypeStruct(s, dtype) if isinstance(s, tuple) else s,
            shape,
            is_leaf=lambda s: isinstance(s, tuple),
        ),
        scratch_shapes=list(scratch),
        compiler_params=PARAMS,
        name=kernel.__name__,
    )


def all_to_all(x, axes):
    return lax.all_to_all(x, axes, split_axis=0, concat_axis=0, tiled=True)


def local(charge, dest, local_ids, green_hat):
    wave, mix = z_tables()
    mix_hi, mix_lo = split_table(mix)
    mix_both = np.concatenate([mix_hi.T, mix_lo.T], axis=0)
    wave_hi, wave_lo = split_table(wave.reshape(9 * 128, 256))
    wave_both = np.concatenate(split_table(wave.transpose(0, 2, 1).reshape(9 * 256, 128)), axis=1)
    x_fwd, x_back = stacked(pair_table(0))
    order = np.arange(64).reshape(N_PZ, CYP).T.reshape(64)
    y_fwd, y_back = (np.stack(tables) for tables in zip(stacked(pair_table(0)), stacked(pair_table(1))))
    y_fwd = y_fwd.reshape(2, 2, 64, 256)[:, :, order].reshape(2, 128, 256)

    charge, dest, local_ids, green_hat = (
        pltpu.with_memory_space_constraint(x, pltpu.HBM)
        for x in (charge, dest.reshape(1, 256), local_ids.reshape(1, 256), green_hat)
    )
    send, place, green_hat = call(
        pack_kernel,
        [(640, 128), (1, 256), (72, 16, 128)],
        [
            pltpu.VMEM((256, 128), F32),
            pltpu.VMEM((1, 256), jnp.int32),
            pltpu.VMEM((1, 256), jnp.int32),
            pltpu.SemaphoreType.DMA((4,)),
        ],
        in_specs=[HBM] * 4,
    )(charge, dest, local_ids, green_hat)
    recv = all_to_all(send.reshape(N_DEV, 1, 640), BOTH).reshape(640, 128)
    tables = [
        pltpu.with_memory_space_constraint(jnp.asarray(x), pltpu.HBM)
        for x in (mix_both, wave_both, x_fwd, x_back, y_fwd, y_back)
    ]
    pieces = call(
        green_kernel,
        [pltpu.HBM((80, 128), F32)] * 4,
        [pltpu.VMEM((128, 128), F32), pltpu.VMEM((4, 80, 128), F32), pltpu.SemaphoreType.DMA((4,))],
        out_specs=[HBM] * 4,
    )(green_hat)
    mix_both, wave_both, x_fwd, x_back, y_fwd, y_back = call(
        table_kernel,
        [jax.ShapeDtypeStruct(x.shape, BF) for x in tables],
        [pltpu.SemaphoreType.DMA((6,))],
        in_specs=[HBM] * 6,
    )(*tables)
    green = [pieces[0]]
    for n in range(1, 4):
        pairs = [(i, i // 4 * 4 + ((i % 4) ^ n)) for i in range(N_PX)]
        green.append(lax.ppermute(pieces[n], "px", pairs))
    lines = call(z_forward_kernel, (640, 128), [pltpu.VMEM((512, 128), F32)])(recv, mix_both, wave_both)
    lines, green = lax.optimization_barrier((lines, green))
    planes = all_to_all(lines.reshape(N_DEV, 1, 640), BOTH).reshape(640, 128)
    planes = call(
        plane_kernel,
        (512, 128),
        [
            pltpu.VMEM((9, 64, 128), F32),
            pltpu.VMEM((16, 64, 128), F32),
            pltpu.VMEM((16, 64, 128), F32),
        ],
    )(planes, *green, x_fwd, x_back, y_fwd, y_back)
    lines = all_to_all(planes.reshape(N_DEV, 4, 128), BOTH).reshape(512, 128)
    rows = call(z_back_kernel, (512, 128), [pltpu.VMEM((512, 128), F32), pltpu.VMEM((1024, 128), F32)])(
        lines, recv, wave_hi, wave_lo, mix_hi, mix_lo
    )
    rows = all_to_all(rows.reshape(N_DEV, 4, 128), BOTH).reshape(512, 128)
    return call(unpack_kernel, (256, 128))(rows, place)


def solution(mesh):
    return jax.shard_map(
        local,
        mesh=mesh,
        in_specs=(
            P(BOTH, None),
            P(BOTH, None),
            P(BOTH),
            P(None, "px", "pz"),
        ),
        out_specs=P(BOTH, None),
        check_vma=False,
    )
```

```python
import jax
import jax.numpy as jnp
import ml_dtypes
import numpy as np
from jax import lax
from jax.experimental import pallas as pl
from jax.experimental.pallas import tpu as pltpu
from jax.sharding import PartitionSpec as P

CXP = 8
CYP = 4
CAP = 4
N_PX = 8
N_PZ = 16
N_DEV = 128
BOTH = ("px", "pz")
RESIDUE = [0, 8] + [g for g in range(1, 8) for _ in range(2)]
BF = jnp.bfloat16
F32 = jnp.float32
VMEM = pl.BlockSpec(memory_space=pltpu.VMEM)
HBM = pl.BlockSpec(memory_space=pltpu.HBM)
PARAMS = pltpu.CompilerParams(vmem_limit_bytes=16 << 20)


def split_table(table):
    high = table.astype(np.float32).astype(ml_dtypes.bfloat16)
    low = (table - high.astype(np.float64)).astype(ml_dtypes.bfloat16)
    return high, low


def z_tables():
    device = np.arange(N_DEV)
    q = 8 * (device % N_PZ) + device // N_PZ
    l = np.arange(128)
    wave = []
    for r in range(9):
        angle = 2.0 * np.pi * ((q[:, None] * 16 + r) * l[None, :] % 2048) / 2048.0
        wave.append(np.concatenate([np.cos(angle), np.sin(angle)], axis=1))
    wave = np.stack(wave)
    mix = np.zeros((8, 4, 8, 2, 4, 16, 8))
    for c in range(8):
        for kk in range(16):
            r = RESIDUE[kk]
            angle = 2.0 * np.pi * ((r * c) % 16) / 16.0
            if kk < 2:
                cosine_part, sine_part, weight = np.cos(angle), np.cos(angle), 1.0
            elif kk % 2 == 0:
                cosine_part, sine_part, weight = np.cos(angle), -np.sin(angle), 2.0
            else:
                cosine_part, sine_part, weight = np.sin(angle), np.cos(angle), 2.0
            scale = np.sqrt(weight / 2048.0)
            for b in range(4):
                for a in range(8):
                    mix[c, b, a, 0, b, kk, a] = cosine_part * scale
                    mix[c, b, a, 1, b, kk, a] = sine_part * scale
    return wave, mix.reshape(256, 1024)


def pair_table(half):
    k = 64 * half + np.arange(64)
    cell = np.arange(64)[:, None]
    cosine = np.cos(2.0 * np.pi * (cell * k[None, :] % 128) / 128.0) * np.sqrt(2.0)
    sine = np.sin(2.0 * np.pi * (cell * k[None, :] % 128) / 128.0) * np.sqrt(2.0)
    cosine[:, 0] = np.cos(np.pi * half * np.arange(64))
    sine[:, 0] = np.cos(np.pi * (1 - half) * np.arange(64))
    return np.concatenate([cosine, sine], axis=1) / np.sqrt(128.0)


def stacked(table):
    high, low = split_table(table)
    none = np.zeros_like(low)
    fwd = np.block([[high, low], [high, none]])
    back = np.block([[high.T, low.T], [high.T, none.T]])
    return fwd, back


def iota(shape, axis):
    return lax.broadcasted_iota(jnp.int32, shape, axis)


def two(x):
    high = x.astype(BF)
    return high, (x - high.astype(F32)).astype(BF)


def three(x):
    high = x.astype(BF)
    rest = x - high.astype(F32)
    middle = rest.astype(BF)
    return high, middle, (rest - middle.astype(F32)).astype(BF)


def turned_pair(x):
    high = x.astype(BF).astype(F32)
    return jnp.concatenate([high, x - high], axis=0).T.astype(BF)


def halves(x, size):
    return x[:, :size] + x[:, size:]


def dot(a, b, a_axis=1, b_axis=0):
    return lax.dot_general(a, b, (((a_axis,), (b_axis,)), ((), ())), preferred_element_type=F32)


def pack_kernel(
    charge_any, dest_any, ids_any, green_any, send_ref, place_ref, green_ref, charge_ref, dest_ref, ids_ref, sems
):
    moves = [
        pltpu.make_async_copy(source, target, sems.at[n])
        for n, (source, target) in enumerate(
            [
                (dest_any, dest_ref),
                (ids_any, ids_ref),
                (charge_any, charge_ref),
                (green_any.at[:72], green_ref),
            ]
        )
    ]
    for move in moves:
        move.start()
    moves[0].wait()
    dest = jnp.broadcast_to(dest_ref[...], (256, 256))
    row, col = iota((256, 256), 0), iota((256, 256), 1)
    dest_f = dest.astype(F32)
    dest_col = jnp.sum(jnp.where(row == col, dest_f, 0.0), axis=1, keepdims=True)
    earlier = (dest_col == dest_f) & (row < col)
    rank = jnp.sum(jnp.where(earlier, 1.0, 0.0), axis=0, keepdims=True)
    place_ref[...] = dest_f[0:1] * CAP + rank
    here = iota((128, 256), 0) == dest[:128]
    rank = jnp.broadcast_to(rank, (128, 256))
    moves[1].wait()
    ids = jnp.broadcast_to(ids_ref[...], (128, 256)).astype(F32)
    lane = iota((128, 128), 1)
    named = jnp.zeros((128, 128), F32)
    hots = []
    for slot in range(CAP):
        chosen = here & (rank == slot)
        hots.append(jnp.where(chosen, 1.0, 0.0).astype(BF))
        number = jnp.sum(jnp.where(chosen, ids + 1.0, 0.0), axis=1, keepdims=True) - 1.0
        named = jnp.where(lane == 9 + slot, number, named)
    moves[2].wait()
    parts = jnp.concatenate(three(charge_ref[...]), axis=1)
    moved = dot(jnp.concatenate(hots, axis=0), parts)
    moved = moved[:, :128] + moved[:, 128:256] + moved[:, 256:]
    for slot in range(CAP):
        send_ref[pl.ds(slot, 128, stride=5), :] = moved[slot * 128 : (slot + 1) * 128]
    moves[3].wait()
    plane = jnp.concatenate([green_ref[:, 0, :], jnp.zeros((56, 128), F32)], axis=0)
    send_ref[pl.ds(4, 128, stride=5), :] = jnp.where((lane >= 9) & (lane < 9 + CAP), named, plane)


def block_name(index):
    return (((index % 8) * 4 + (index // 8) % 4) * 8 + index // 32).astype(F32)


def slot_rows(r):
    first, count = (0, 8) if r == 0 else (8, 8) if r == 8 else (16 * r, 16)
    return [slice(b * 128 + first, b * 128 + first + count) for b in range(CYP)], count


def z_forward_kernel(recv_ref, mix_ref, wave_ref, out_ref, turned_ref):
    ends = recv_ref[pl.ds(4, 128, stride=5), :]
    names = ends.T
    block = block_name(iota((256, 128), 0))
    hots = [jnp.where(block == names[9 + s : 10 + s, :], 1.0, 0.0).astype(BF) for s in range(CAP)]
    rows = jnp.concatenate([recv_ref[pl.ds(s, 128, stride=5), :] for s in range(CAP)], axis=0)
    field = dot(jnp.concatenate(hots, axis=1), jnp.concatenate(three(rows), axis=1))
    field = field[:, :128] + field[:, 128:256] + field[:, 256:]
    high, low = two(field)
    mixed = dot(mix_ref[:1024], jnp.concatenate([high, low], axis=1))
    mixed = mixed[:, :128] + mixed[:, 128:] + dot(mix_ref[1024:], high)
    mixed = jnp.concatenate([mixed[:512], mixed[512:]], axis=1)
    for r in range(9):
        places, count = slot_rows(r)
        high, low = two(jnp.concatenate([mixed[place] for place in places], axis=0))
        block = dot(jnp.concatenate([high, low], axis=0), wave_ref[r * 256 : (r + 1) * 256, :])
        size = 4 * count
        block = block[:size, :128] + block[:size, 128:] + block[size:, :128]
        for b, place in enumerate(places):
            turned_ref[place, :] = block[b * count : (b + 1) * count]
    for b in range(CYP):
        out_ref[pl.ds(b, 128, stride=5), :] = turned_ref[b * 128 : (b + 1) * 128, :].T
    relayed = []
    for i in range(N_PX):
        source = 64 if i < 4 else 0
        rows = ends[source : source + 16]
        relayed.append(pltpu.roll(rows, 128 - 16 * i, 1) if i else rows)
    out_ref[pl.ds(4, 128, stride=5), :] = jnp.concatenate(relayed, axis=0)


def plane_kernel(spec_ref, *refs):
    pieces, refs = refs[:4], refs[4:]
    x_fwd_ref, x_back_ref, y_fwd_ref, y_back_ref, out_ref, green_ref, first_ref, second_ref = refs
    me = lax.axis_index("px")
    half, place = me // 4, me % 4
    left, middle = iota((8, 128), 1) < 64, iota((8, 128), 1) == 64
    for n in range(4):
        start = pl.multiple_of(jnp.bitwise_xor(place, n) * 16, 16)
        last = pieces[n][72:80, :]
        for r in range(9):
            pair = pieces[n][r * 8 : (r + 1) * 8, :]
            swapped = pltpu.roll(pair, 64, 1)
            low = jnp.where(middle, last[:, r : r + 1], jnp.where(left, pair, swapped))
            high = jnp.where(middle, last[:, 64 + r : 65 + r], jnp.where(left, swapped, pair))
            green_ref[r, pl.ds(start, 16), :] = jnp.concatenate([low, high], axis=0)
    ends = spec_ref[pl.ds(4, 128, stride=5), :].T[:16]
    lane = iota((16, 128), 1)
    ends = jnp.where(lane <= 64, ends, pltpu.roll(ends, 64, 1))
    y_fwd, y_back, x_fwd, x_back = y_fwd_ref[half], y_back_ref[half], x_fwd_ref[...], x_back_ref[...]
    for pair in range(4):
        rows = []
        for i in (2 * pair, 2 * pair + 1):
            cells = [spec_ref[pl.ds(i * 80 + b, 16, stride=5), :] for b in range(CYP)]
            rows.append(turned_pair(jnp.concatenate(cells, axis=0)))
        turned = halves(dot(jnp.concatenate(rows, axis=0), y_fwd), 128)
        for kk in range(16):
            first_ref[kk, pair * 16 : pair * 16 + 8, :] = turned[kk * 8 : kk * 8 + 8]
            first_ref[kk, pair * 16 + 8 : pair * 16 + 16, :] = turned[128 + kk * 8 : 136 + kk * 8]
    top = iota((64, 128), 0) == 0
    for group in range(4):
        rows = jnp.concatenate([turned_pair(first_ref[group * 4 + n]) for n in range(4)], axis=0)
        full = halves(dot(rows, x_fwd), 128)
        scaled = []
        for n in range(4):
            r = RESIDUE[group * 4 + n]
            green = green_ref[r]
            other = jnp.where(top, ends[r : r + 1, :], green)
            scaled += [full[n * 128 : n * 128 + 64] * green, full[n * 128 + 64 : (n + 1) * 128] * other]
        high, low = two(jnp.concatenate(scaled, axis=0))
        cells = dot(jnp.concatenate([high, low], axis=1), x_back)
        for n in range(4):
            pair = cells[n * 128 : (n + 1) * 128].T
            second_ref[group * 4 + n] = pair[:64] + pair[64:]
    for pair in range(4):
        rows = [
            second_ref[kk, i * 8 : (i + 1) * 8, :] for i in (2 * pair, 2 * pair + 1) for kk in range(16)
        ]
        high, low = two(jnp.concatenate(rows, axis=0))
        cells = dot(y_back, jnp.concatenate([high, low], axis=1), 0, 1)
        cells = cells[:64] + cells[64:]
        out_ref[pair * 128 : pair * 128 + 64, :] = cells[:, :128]
        out_ref[pair * 128 + 64 : pair * 128 + 128, :] = cells[:, 128:]


def z_back_kernel(spec_ref, recv_ref, wave_hi_ref, wave_lo_ref, mix_hi_ref, mix_lo_ref, out_ref, turned_ref, line_ref):
    for b in range(CYP):
        turned_ref[b * 128 : (b + 1) * 128, :] = spec_ref[pl.ds(b, 128, stride=4), :].T
    for r in range(9):
        places, count = slot_rows(r)
        high, low = two(jnp.concatenate([turned_ref[place, :] for place in places], axis=0))
        rows = slice(r * 128, (r + 1) * 128)
        size = 4 * count
        block = dot(jnp.concatenate([high, low], axis=0), wave_hi_ref[rows, :])
        block = block[:size] + block[size:] + dot(high, wave_lo_ref[rows, :])
        for b, place in enumerate(places):
            part = block[b * count : (b + 1) * count]
            line_ref[place, :] = part[:, :128]
            line_ref[slice(place.start + 512, place.stop + 512), :] = part[:, 128:]
    high, low = two(line_ref[...])
    field = dot(mix_hi_ref[...], jnp.concatenate([high, low], axis=1))
    field = field[:, :128] + field[:, 128:] + dot(mix_lo_ref[...], high)
    block = block_name(iota((128, 256), 1))
    names = recv_ref[pl.ds(4, 128, stride=5), :]
    hots = [jnp.where(names[:, 9 + s : 10 + s] == block, 1.0, 0.0).astype(BF) for s in range(CAP)]
    rows = dot(jnp.concatenate(hots, axis=0), jnp.concatenate(three(field), axis=1))
    rows = rows[:, :128] + rows[:, 128:256] + rows[:, 256:]
    for s in range(CAP):
        out_ref[pl.ds(s, 128, stride=4), :] = rows[s * 128 : (s + 1) * 128]


def unpack_kernel(back_ref, place_ref, out_ref):
    row, col = iota((256, 256), 0), iota((256, 256), 1)
    place = jnp.broadcast_to(place_ref[...], (256, 256))
    place = jnp.sum(jnp.where(row == col, place, 0.0), axis=1, keepdims=True).astype(jnp.int32)
    hots = jnp.where(iota((256, 512), 1) == place, 1.0, 0.0).astype(BF)
    parts = jnp.concatenate(three(back_ref[...]), axis=1)
    rows = dot(hots, parts)
    out_ref[...] = rows[:, :128] + rows[:, 128:256] + rows[:, 256:]


def green_kernel(green_ref, *refs):
    out_refs, (turned_ref, piece_ref, sems) = refs[:4], refs[4:]
    me = lax.axis_index("px")
    starts = [
        pl.multiple_of((me - me % 4 + jnp.bitwise_xor(me % 4, n)) * 16, 16) for n in range(4)
    ]
    left = iota((8, 128), 1) < 64
    for k2 in range(8):
        both = jnp.concatenate([green_ref[:64, k2, :], green_ref[:64, k2 + 8, :]], axis=0)
        turned_ref[...] = both.T
        for n in range(4):
            piece_ref[n, pl.ds(k2, 8, stride=8), :] = turned_ref[pl.ds(starts[n], 8), :]
            piece_ref[n, 64 + k2 : 65 + k2, :] = turned_ref[pl.ds(starts[n] + 8, 1), :]
    middle = green_ref[64]
    for n in range(4):
        low = pltpu.roll(middle[:8], 128 - starts[n], 1)
        high = pltpu.roll(middle[8:], 192 - starts[n], 1)
        piece_ref[n, 72:80, :] = jnp.where(left, low, high)
    stores = [pltpu.make_async_copy(piece_ref.at[n], out_refs[n], sems.at[n]) for n in range(4)]
    for move in stores:
        move.start()
    for move in stores:
        move.wait()


def table_kernel(*refs):
    tables, copies, sems = refs[:6], refs[6:12], refs[12]
    moves = [pltpu.make_async_copy(tables[n], copies[n], sems.at[n]) for n in range(6)]
    for move in moves:
        move.start()
    for move in moves:
        move.wait()


def call(kernel, shape, scratch=(), dtype=F32, **specs):
    return pl.pallas_call(
        kernel,
        **specs,
        out_shape=jax.tree.map(
            lambda s: jax.ShapeDtypeStruct(s, dtype) if isinstance(s, tuple) else s,
            shape,
            is_leaf=lambda s: isinstance(s, tuple),
        ),
        scratch_shapes=list(scratch),
        compiler_params=PARAMS,
        name=kernel.__name__,
    )


def all_to_all(x, axes):
    return lax.all_to_all(x, axes, split_axis=0, concat_axis=0, tiled=True)


def local(charge, dest, local_ids, green_hat):
    wave, mix = z_tables()
    mix_hi, mix_lo = split_table(mix)
    mix_both = np.concatenate([mix_hi.T, mix_lo.T], axis=0)
    wave_hi, wave_lo = split_table(wave.reshape(9 * 128, 256))
    wave_both = np.concatenate(split_table(wave.transpose(0, 2, 1).reshape(9 * 256, 128)), axis=1)
    x_fwd, x_back = stacked(pair_table(0))
    order = np.arange(64).reshape(N_PZ, CYP).T.reshape(64)
    y_fwd, y_back = (np.stack(tables) for tables in zip(stacked(pair_table(0)), stacked(pair_table(1))))
    y_fwd = y_fwd.reshape(2, 2, 64, 256)[:, :, order].reshape(2, 128, 256)

    charge, dest, local_ids, green_hat = (
        pltpu.with_memory_space_constraint(x, pltpu.HBM)
        for x in (charge, dest.reshape(1, 256), local_ids.reshape(1, 256), green_hat)
    )
    send, place, green_hat = call(
        pack_kernel,
        [(640, 128), (1, 256), (72, 16, 128)],
        [
            pltpu.VMEM((256, 128), F32),
            pltpu.VMEM((1, 256), jnp.int32),
            pltpu.VMEM((1, 256), jnp.int32),
            pltpu.SemaphoreType.DMA((4,)),
        ],
        in_specs=[HBM] * 4,
    )(charge, dest, local_ids, green_hat)
    recv = all_to_all(send.reshape(N_DEV, 1, 640), BOTH).reshape(640, 128)
    tables = [
        pltpu.with_memory_space_constraint(jnp.asarray(x), pltpu.HBM)
        for x in (mix_both, wave_both, x_fwd, x_back, y_fwd, y_back)
    ]
    pieces = call(
        green_kernel,
        [pltpu.HBM((80, 128), F32)] * 4,
        [pltpu.VMEM((128, 128), F32), pltpu.VMEM((4, 80, 128), F32), pltpu.SemaphoreType.DMA((4,))],
        out_specs=[HBM] * 4,
    )(green_hat)
    mix_both, wave_both, x_fwd, x_back, y_fwd, y_back = call(
        table_kernel,
        [jax.ShapeDtypeStruct(x.shape, BF) for x in tables],
        [pltpu.SemaphoreType.DMA((6,))],
        in_specs=[HBM] * 6,
    )(*tables)
    green = [pieces[0]]
    for n in range(1, 4):
        pairs = [(i, i // 4 * 4 + ((i % 4) ^ n)) for i in range(N_PX)]
        green.append(lax.ppermute(pieces[n], "px", pairs))
    lines = call(z_forward_kernel, (640, 128), [pltpu.VMEM((512, 128), F32)])(recv, mix_both, wave_both)
    lines, green = lax.optimization_barrier((lines, green))
    planes = all_to_all(lines.reshape(N_DEV, 1, 640), BOTH).reshape(640, 128)
    planes = call(
        plane_kernel,
        (512, 128),
        [
            pltpu.VMEM((9, 64, 128), F32),
            pltpu.VMEM((16, 64, 128), F32),
            pltpu.VMEM((16, 64, 128), F32),
        ],
    )(planes, *green, x_fwd, x_back, y_fwd, y_back)
    lines = all_to_all(planes.reshape(N_DEV, 4, 128), BOTH).reshape(512, 128)
    rows = call(z_back_kernel, (512, 128), [pltpu.VMEM((512, 128), F32), pltpu.VMEM((1024, 128), F32)])(
        lines, recv, wave_hi, wave_lo, mix_hi, mix_lo
    )
    rows = all_to_all(rows.reshape(N_DEV, 4, 128), BOTH).reshape(512, 128)
    return call(unpack_kernel, (256, 128))(rows, place)


def solution(mesh):
    return jax.shard_map(
        local,
        mesh=mesh,
        in_specs=(
            P(BOTH, None),
            P(BOTH, None),
            P(BOTH),
            P(None, "px", "pz"),
        ),
        out_specs=P(BOTH, None),
        check_vma=False,
    )
```
